256 devices in a mesh: dev: 8 (over z), ha: 4 (over y), wa: 8 (over x, core).
Axes of the slice: x: 4, y: 4, z: 8, core: 2. Of those that a mesh axis runs over, the one named last changes fastest.
Arguments:
- volume: float32 [32, 32, 64, 256], P('dev', 'ha', 'wa'), may hold values from -6 to 6
- kernel: float32 [256, 27, 256], replicated, may hold values from -0.078125 to 0.078125
- upstream: float32 [32, 32, 64, 256], P('dev', 'ha', 'wa'), may hold values from -6 to 6
Outputs:
- output: float32 [32, 32, 64, 256], P('dev', 'ha', 'wa')
- volume_grad: float32 [32, 32, 64, 256], P('dev', 'ha', 'wa')
- kernel_grad: float32 [256, 27, 256], P('wa')
The draws below stay inside these ranges and needn't reach their ends.
All inputs are finite; a program needn't handle non-finite values.
Results may differ from the reference program's by a relative error of at most 0.0001.
Values sent between devices are 32-bit elements; how exact they have to be, the bound alone decides.
A program may use at most 128 MiB of HBM per device.

```python
import math
import jax
import jax.numpy as jnp
from jax import lax

C = 256
TAPS = 27
DEPTH = 32
HEIGHT = 32
WIDTH = 64


def shard_levels(key, shape, shards, least, largest):
    def one(position, shards_of):
        draws = jax.random.uniform(jax.random.fold_in(jax.random.fold_in(key, 6), position), (shards_of,), jnp.float32, least / len(shards), largest / len(shards))
        return jnp.repeat(jnp.exp(draws), shape[position] // shards_of).reshape((-1,) + (1,) * (len(shape) - position - 1))

    factor_of = one(*shards[0])
    for cut in shards[1:]:
        factor_of = factor_of * one(*cut)
    return factor_of


def noise(rng, extent, width, reach, split=(), dtype=jnp.bfloat16):
    gain = shard_levels(rng, extent, split, -0.22, 0.18) if split else 1.0
    drawn = jax.random.normal(rng, extent, jnp.float32) * width * gain
    return jnp.minimum(jnp.maximum(drawn, -reach), reach).astype(dtype)


def setup_inputs(seed: int = 0) -> dict:
    arg_keys = jax.random.split(jax.random.key(seed), 4)
    volume = noise(arg_keys[0], (DEPTH, HEIGHT, WIDTH, C), 1.0, 6.0, ((0, 8), (1, 4), (2, 8)), jnp.float32)
    kernel = noise(arg_keys[1], (C, TAPS, C), (C * TAPS) ** -0.5, 0.078125, (), jnp.float32)
    upstream = noise(arg_keys[2], (DEPTH, HEIGHT, WIDTH, C), 1.0, 6.0, ((0, 8), (1, 4), (2, 8)), jnp.float32)
    return dict(volume=volume, kernel=kernel, upstream=upstream)


def tap_offsets():
    return [(da, db, dc) for da in (-1, 0, 1) for db in (-1, 0, 1) for dc in (-1, 0, 1)]

def reference(volume, kernel, upstream):
    cells = DEPTH * HEIGHT * WIDTH
    flat_up = upstream.reshape(cells, C)
    output = jnp.zeros((cells, C), jnp.float32)
    volume_grad = jnp.zeros((cells, C), jnp.float32)
    grads = []
    for tap_index, (da, db, dc) in enumerate(tap_offsets()):
        shifted = jnp.roll(volume, (-da, -db, -dc), axis=(0, 1, 2)).reshape(cells, C)
        weight = kernel[:, tap_index, :]
        output = output + jnp.dot(shifted, weight, precision=lax.Precision.HIGHEST, preferred_element_type=jnp.float32)
        back = jnp.roll(upstream, (da, db, dc), axis=(0, 1, 2)).reshape(cells, C)
        volume_grad = volume_grad + jnp.dot(back, weight.T, precision=lax.Precision.HIGHEST, preferred_element_type=jnp.float32)
        grads.append(jnp.dot(shifted.T, flat_up, precision=lax.Precision.HIGHEST, preferred_element_type=jnp.float32))
    kernel_grad = jnp.stack(grads, axis=1) * (1.0 / math.sqrt(cells))
    return (output.reshape(DEPTH, HEIGHT, WIDTH, C), volume_grad.reshape(DEPTH, HEIGHT, WIDTH, C), kernel_grad)
```

```python
import functools
import math

import jax
import jax.numpy as jnp
from jax import lax
from jax.experimental import pallas as pl
from jax.experimental.pallas import tpu as pltpu
from jax.sharding import PartitionSpec as P

MESH = pl.DeviceIdType.MESH
F32 = jnp.float32
BF16 = jnp.bfloat16

GROUPS = 7
FIRST = ("x", "y", "x", "y", "x", "y", "x")
BATCHES = ((0, 4), (4, 7))
N_SEM = 2 * 10 + GROUPS + GROUPS * 8 + len(BATCHES) * (7 + 7 + 4)


def split(x):
    hi = x.astype(BF16)
    return hi, (x - hi.astype(F32)).astype(BF16)


def dot3(lhs, rhs, dims):
    (lh, ll), (rh, rl) = lhs, rhs
    dot = functools.partial(
        lax.dot_general, dimension_numbers=(dims, ((), ())), preferred_element_type=F32
    )
    return dot(lh, rh) + (dot(ll, rh) + dot(lh, rl))


def kernel(
    factor,
    vol_ref, up_ref, k_hbm, out_ref, vg_ref, kg_ref,
    k_f, pad_v, pad_u, col_v, col_u, halo_v, halo_u,
    wv_hi, wv_lo, wu_hi, wu_lo, vt_hi, vt_lo, acc_o, acc_g,
    part, pair, summed, r1, s2, r2, mid, q1, t2, q2, low, rz, fin, agz, full,
    ksem, send_sem, recv_sem,
):
    z, y, w = lax.axis_index("dev"), lax.axis_index("ha"), lax.axis_index("wa")
    core = lax.rem(w, 2)
    x = lax.div(w, 2)

    def step(i, by, n):
        return lax.rem(i + (by + n), n)

    counter = [0]
    sent = []

    def copy(src, dst, device):
        i = counter[0]
        counter[0] += 1
        return pltpu.make_async_remote_copy(
            src_ref=src, dst_ref=dst, send_sem=send_sem.at[i], recv_sem=recv_sem.at[i],
            device_id=device, device_id_type=MESH,
        )

    def start(*copies):
        for c in copies:
            c.start()
            sent.append(c)
        return copies

    k_copies = [
        pltpu.make_async_copy(k_hbm.at[pl.ds(9 * i, 9)], k_f.at[pl.ds(9 * i, 9)], ksem.at[i])
        for i in range(3)
    ]
    for c in k_copies:
        c.start()

    peers = []
    for sd in (-1, 0, 1):
        for sh in (-1, 0, 1):
            if (sd, sh) != (0, 0):
                peers.append({"dev": step(z, sd, 8), "ha": step(y, sh, 4)})
    for k in range(2, 7):
        peers.append({"dev": step(z, k, 8)})
    for k in (-2, -1, 1, 2):
        peers.append({"wa": step(w, k, 8)})
    barrier = pltpu.get_barrier_semaphore()
    for peer in peers:
        pl.semaphore_signal(barrier, inc=1, device_id=peer, device_id_type=MESH)
    pad_u[1:5, 1:9] = up_ref[...]
    pad_v[1:5, 1:9] = vol_ref[...]
    pl.semaphore_wait(barrier, len(peers))

    def send_faces(src, pad):
        copies = []
        for sd in (-1, 0, 1):
            for sh in (-1, 0, 1):
                if (sd, sh) == (0, 0):
                    continue
                d_src, d_dst, d_n = ((0, 5, 1), (0, 1, 4), (3, 0, 1))[sd + 1]
                h_src, h_dst, h_n = ((0, 9, 1), (0, 1, 8), (7, 0, 1))[sh + 1]
                copies.append(copy(
                    src.at[pl.ds(d_src, d_n), pl.ds(h_src, h_n)],
                    pad.at[pl.ds(d_dst, d_n), pl.ds(h_dst, h_n)],
                    {"dev": step(z, sd, 8), "ha": step(y, sh, 4)},
                ))
        return start(*copies)

    def send_columns(pad, col, halo):
        col[0] = pad[:, :, 0:1, :]
        col[1] = pad[:, :, 7:8, :]
        return start(
            copy(col.at[0], halo.at[1], {"wa": step(w, -1, 8)}),
            copy(col.at[1], halo.at[0], {"wa": step(w, 1, 8)}),
        )

    def arrive(copies):
        for c in copies:
            c.wait_recv()

    def windows(pad, halo, hi_ref, lo_ref):
        def body(d, carry):
            rows = pl.ds(pl.multiple_of(d * 64, 64), 64)
            plane = pad[d]
            at = lax.broadcasted_iota(jnp.int32, plane.shape, 1)
            before = jnp.broadcast_to(halo[0, d], plane.shape)
            after = jnp.broadcast_to(halo[1, d], plane.shape)
            shifted = (
                jnp.where(at == 0, before, pltpu.roll(plane, 1, 1)),
                plane,
                jnp.where(at == 7, after, pltpu.roll(plane, 7, 1)),
            )
            for b in range(3):
                for c in range(3):
                    hi, lo = split(shifted[c][b : b + 8].reshape(64, plane.shape[-1]))
                    hi_ref[3 * b + c, rows, :] = hi
                    lo_ref[3 * b + c, rows, :] = lo
            return carry

        lax.fori_loop(0, 6, body, 0)

    def window(hi_ref, lo_ref, t):
        rows = pl.ds(pl.multiple_of(lax.div(t, 9) * 64, 64), 256)
        i = lax.rem(t, 9)
        return hi_ref[i, rows, :], lo_ref[i, rows, :]

    def kernel_grad(g):
        def body(i, carry):
            t = 4 * g + i
            upwin = window(wu_hi, wu_lo, 26 - t)
            res = dot3((vt_hi[...], vt_lo[...]), upwin, ((1,), (0,)))
            for block in range(8):
                for half in range(2):
                    part[g, block % 2, block // 2, 2 * i + half] = res[
                        32 * block : 32 * block + 32, 128 * half : 128 * half + 128
                    ]
            return carry

        taps = min(4, 27 - 4 * g)
        lax.fori_loop(0, taps, body, 0)
        for i in range(taps, 4):
            for j in (2 * i, 2 * i + 1):
                part[g, :, :, j] = jnp.zeros((2, 4, 32, 128), F32)

    def products(first, last):
        def body(t, carry):
            k = split(k_f[t])
            acc_o[...] += dot3(window(wv_hi, wv_lo, t), k, ((1,), (0,)))
            acc_g[...] += dot3(window(wu_hi, wu_lo, 26 - t), k, ((1,), (1,)))
            return carry

        lax.fori_loop(first, last, body, 0)

    def ring_devices(axis):
        if axis == "x":
            return x, {"wa": step(w, 2, 8)}, {"wa": step(w, -2, 8)}
        return y, {"ha": step(y, 1, 4)}, {"ha": step(y, -1, 4)}

    def ring_1(axis, chunk, recv):
        i, up, down = ring_devices(axis)
        far = chunk(step(i, 2, 4))
        return start(
            copy(halves(far, 0), recv.at[0], up),
            copy(halves(far, 1), recv.at[1], down),
        )

    def halves(ref, h):
        if len(ref.shape) == 4:
            return ref.at[:, pl.ds(4 * h, 4)]
        return ref.at[pl.ds(4 * h, 4)]

    def ring_2(axis, copies, chunk, recv, stage, recv_2):
        i, up, down = ring_devices(axis)
        arrive(copies)
        for h, by in ((0, 1), (1, -1)):
            near = chunk(step(i, by, 4))
            halves(stage.at[h], h)[...] = halves(near, h)[...] + recv[h]
            halves(stage.at[h], 1 - h)[...] = halves(near, 1 - h)[...]
        return start(copy(stage.at[0], recv_2.at[0], up), copy(stage.at[1], recv_2.at[1], down))

    def ring_3(axis, copies, chunk, recv_2):
        i, _, _ = ring_devices(axis)
        arrive(copies)
        return chunk(i)[...] + recv_2[0] + recv_2[1]

    def rows_of(ref, k):
        rows = pl.ds(pl.multiple_of(k * 8, 8), 8)
        if len(ref.shape) == 4:
            return ref.at[:, :, rows]
        return ref.at[:, rows]

    class Group:
        def __init__(self, g):
            self.g = g
            self.first = FIRST[g]
            self.second = "y" if self.first == "x" else "x"
            n = FIRST[:g].count(self.first)
            i = 0 if self.first == "x" else 1
            self.r1, self.s2, self.r2 = r1[i].at[n], s2[i].at[n], r2[i].at[n]
            self.mid = mid[i].at[n]
            self.sum = summed.at[g]
            self.q1, self.t2, self.q2 = q1.at[g], t2.at[g], q2.at[g]
            if self.first == "x":
                self.chunk_1 = lambda k: self.sum.at[k]
                self.chunk_2 = lambda k: rows_of(self.mid, k)
            else:
                self.chunk_1 = lambda k: rows_of(self.sum, k)
                self.chunk_2 = lambda k: self.mid.at[k]

        def pair(self):
            self.c = start(copy(part.at[self.g, 1 - core], pair.at[self.g], {"wa": w + 1 - 2 * core}))

        def e1(self):
            arrive(self.c)
            self.sum[...] = part[self.g, core] + pair[self.g]
            self.c = ring_1(self.first, self.chunk_1, self.r1)

        def e2(self):
            self.c = ring_2(self.first, self.c, self.chunk_1, self.r1, self.s2, self.r2)

        def e3(self):
            self.mid[...] = ring_3(self.first, self.c, self.chunk_1, self.r2)
            self.c = ring_1(self.second, self.chunk_2, self.q1)

        def e4(self):
            self.c = ring_2(self.second, self.c, self.chunk_2, self.q1, self.t2, self.q2)

        def e5(self):
            low[self.g] = ring_3(self.second, self.c, self.chunk_2, self.q2)

    class Batch:
        def __init__(self, i):
            self.lo, self.hi = BATCHES[i]
            self.gs = pl.ds(self.lo, self.hi - self.lo)

        def e6(self):
            self.c = start(*(
                copy(low.at[self.gs, step(z, k, 8)], rz.at[k - 1, self.gs], {"dev": step(z, k, 8)})
                for k in range(1, 8)
            ))

        def e7(self):
            arrive(self.c)
            total = low[self.gs, z]
            for k in range(7):
                total = total + rz[k, self.gs]
            total = total * factor
            fin[self.gs] = total
            agz[self.gs, z] = total
            sends, self.c = [], []
            for k in range(1, 8):
                i = counter[0]
                sends.append(copy(fin.at[self.gs], agz.at[self.gs, z], {"dev": step(z, k, 8)}))
                self.c.append(pltpu.make_async_remote_copy(
                    src_ref=fin.at[self.gs], dst_ref=agz.at[self.gs, step(z, -k, 8)],
                    send_sem=send_sem.at[i], recv_sem=recv_sem.at[i],
                    device_id={"dev": step(z, k, 8)}, device_id_type=MESH,
                ))
            start(*sends)

        def landed(self, sends, slots):
            return [
                pltpu.make_async_remote_copy(
                    src_ref=slot, dst_ref=slot, send_sem=send_sem.at[i], recv_sem=recv_sem.at[i],
                    device_id={"ha": step(y, 1, 4)}, device_id_type=MESH,
                )
                for i, slot in zip(sends, slots)
            ]

        def e8(self):
            arrive(self.c)
            full[self.gs, :, y] = agz[self.gs]
            i = counter[0]
            mine = full.at[self.gs, :, y]
            start(
                copy(agz.at[self.gs], mine, {"ha": step(y, 1, 4)}),
                copy(agz.at[self.gs], mine, {"ha": step(y, -1, 4)}),
            )
            self.c = self.landed(
                (i, i + 1), (full.at[self.gs, :, step(y, -1, 4)], full.at[self.gs, :, step(y, 1, 4)])
            )

        def e9(self):
            arrive(self.c)
            i = counter[0]
            below = full.at[self.gs, pl.ds(0, 4), step(y, -1, 4)]
            above = full.at[self.gs, pl.ds(4, 4), step(y, 1, 4)]
            start(
                copy(below, below, {"ha": step(y, 1, 4)}),
                copy(above, above, {"ha": step(y, -1, 4)}),
            )
            far = step(y, 2, 4)
            self.c = self.landed(
                (i, i + 1), (full.at[self.gs, pl.ds(0, 4), far], full.at[self.gs, pl.ds(4, 4), far])
            )

        def e10(self):
            arrive(self.c)
            for g in range(self.lo, self.hi):
                for t in range(4 * g, min(4 * g + 4, 27)):
                    for half in range(2):
                        kg_ref[t, :, 128 * half : 128 * half + 128] = full[
                            g, 2 * (t - 4 * g) + half
                        ].reshape(32, 128)

    faces_u = send_faces(up_ref, pad_u)
    faces_v = send_faces(vol_ref, pad_v)
    hi, lo = split(vol_ref[...].reshape(256, 256).T)
    vt_hi[...] = hi
    vt_lo[...] = lo
    acc_o[...] = jnp.zeros_like(acc_o)
    acc_g[...] = jnp.zeros_like(acc_g)
    arrive(faces_u)
    cols_u = send_columns(pad_u, col_u, halo_u)
    arrive(faces_v)
    cols_v = send_columns(pad_v, col_v, halo_v)
    arrive(cols_u)
    windows(pad_u, halo_u, wu_hi, wu_lo)

    groups = [Group(g) for g in range(GROUPS)]
    batches = [Batch(i) for i in range(len(BATCHES))]
    for g in range(GROUPS):
        kernel_grad(g)
        groups[g].pair()
        if g >= 1:
            groups[g - 1].e1()
        if g >= 3:
            groups[g - 3].e2()
    groups[6].e1()
    arrive(cols_v)
    windows(pad_v, halo_v, wv_hi, wv_lo)
    for c in k_copies:
        c.wait()
    groups[4].e2()
    groups[0].e3()
    groups[1].e3()
    products(0, 5)
    groups[5].e2()
    groups[6].e2()
    groups[0].e4()
    groups[1].e4()
    products(5, 11)
    groups[2].e3()
    groups[3].e3()
    groups[0].e5()
    groups[1].e5()
    products(11, 16)
    groups[2].e4()
    groups[3].e4()
    products(16, 21)
    groups[4].e3()
    groups[5].e3()
    groups[2].e5()
    groups[3].e5()
    batches[0].e6()
    products(21, 27)
    out_ref[...] = acc_o[...].reshape(out_ref.shape)
    vg_ref[...] = acc_g[...].reshape(vg_ref.shape)
    groups[4].e4()
    groups[5].e4()
    groups[6].e3()
    batches[0].e7()
    groups[4].e5()
    groups[5].e5()
    groups[6].e4()
    batches[0].e8()
    groups[6].e5()
    batches[1].e6()
    batches[0].e9()
    batches[1].e7()
    batches[0].e10()
    batches[1].e8()
    batches[1].e9()
    batches[1].e10()
    assert counter[0] == N_SEM, counter[0]
    for c in sent:
        c.wait_send()


def per_device(factor, volume, kernel_taps, upstream):
    nx, ny = FIRST.count("x"), FIRST.count("y")
    vmem = pltpu.VMEM

    def both(tail, n_last=None):
        return tail

    scratch = [
        vmem((27, 256, 256), F32),
        vmem((6, 10, 8, 256), F32), vmem((6, 10, 8, 256), F32),
        vmem((2, 6, 10, 1, 256), F32), vmem((2, 6, 10, 1, 256), F32),
        vmem((2, 6, 10, 1, 256), F32), vmem((2, 6, 10, 1, 256), F32),
        vmem((9, 384, 256), BF16), vmem((9, 384, 256), BF16),
        vmem((9, 384, 256), BF16), vmem((9, 384, 256), BF16),
        vmem((256, 256), BF16), vmem((256, 256), BF16),
        vmem((256, 256), F32), vmem((256, 256), F32),
        vmem((GROUPS, 2, 4, 8, 32, 128), F32),
        vmem((GROUPS, 4, 8, 32, 128), F32),
        vmem((GROUPS, 4, 8, 32, 128), F32),
        [vmem((nx, 2, 4, 32, 128), F32), vmem((ny, 2, 4, 4, 8, 128), F32)],
        [vmem((nx, 2, 8, 32, 128), F32), vmem((ny, 2, 4, 8, 8, 128), F32)],
        [vmem((nx, 2, 8, 32, 128), F32), vmem((ny, 2, 4, 8, 8, 128), F32)],
        [vmem((nx, 8, 32, 128), F32), vmem((ny, 4, 8, 8, 128), F32)],
        vmem((GROUPS, 2, 4, 8, 128), F32),
        vmem((GROUPS, 2, 8, 8, 128), F32),
        vmem((GROUPS, 2, 8, 8, 128), F32),
        vmem((GROUPS, 8, 8, 128), F32),
        vmem((7, GROUPS, 8, 128), F32),
        vmem((GROUPS, 8, 128), F32),
        vmem((GROUPS, 8, 8, 128), F32),
        vmem((GROUPS, 8, 4, 8, 128), F32),
        pltpu.SemaphoreType.DMA((3,)),
        pltpu.SemaphoreType.DMA((N_SEM,)),
        pltpu.SemaphoreType.DMA((N_SEM,)),
    ]
    in_vmem = pl.BlockSpec(memory_space=pltpu.VMEM)
    output, volume_grad, kg = pl.pallas_call(
        functools.partial(kernel, factor),
        out_shape=(
            jax.ShapeDtypeStruct(volume.shape, F32),
            jax.ShapeDtypeStruct(volume.shape, F32),
            jax.ShapeDtypeStruct((27, 32, 256), F32),
        ),
        in_specs=[in_vmem, in_vmem, pl.BlockSpec(memory_space=pl.ANY)],
        out_specs=(in_vmem, in_vmem, in_vmem),
        scratch_shapes=scratch,
        compiler_params=pltpu.CompilerParams(
            collective_id=0, has_side_effects=True, vmem_limit_bytes=56 * 2**20
        ),
    )(volume, upstream, jnp.transpose(kernel_taps, (1, 0, 2)))
    return output, volume_grad, jnp.transpose(kg, (1, 0, 2))


def solution(mesh):
    cells = 256 * mesh.shape["dev"] * mesh.shape["ha"] * mesh.shape["wa"]
    place = P("dev", "ha", "wa", None)
    return jax.shard_map(
        functools.partial(per_device, 1.0 / math.sqrt(cells)),
        mesh=mesh,
        in_specs=(place, P(), place),
        out_specs=(place, place, P("wa", None, None)),
        check_vma=False,
    )
```

```python
import functools
import math

import jax
import jax.numpy as jnp
from jax import lax
from jax.experimental import pallas as pl
from jax.experimental.pallas import tpu as pltpu
from jax.sharding import PartitionSpec as P

MESH = pl.DeviceIdType.MESH
F32 = jnp.float32
BF16 = jnp.bfloat16

GROUPS = 7
FIRST = ("z", "x", "y", "x", "y", "x", "y")
BATCHES = ((0, 4), (4, 7))
N_SEM = 2 * 10 + GROUPS + 6 * (2 + 2 + 3) + (7 + 3 + 3) + len(BATCHES) * (7 + 7 + 3)


def tap(u):
    if isinstance(u, int):
        return 3 * u + 1 if u < 9 else 3 * ((u - 9) // 2) + 2 * ((u - 9) % 2)
    v = jnp.maximum(u - 9, 0)
    return jnp.where(u < 9, 3 * u + 1, 3 * lax.div(v, 2) + 2 * lax.rem(v, 2))


def split(x):
    hi = x.astype(BF16)
    return hi, (x - hi.astype(F32)).astype(BF16)


def dot3(lhs, rhs, dims):
    (lh, ll), (rh, rl) = lhs, rhs
    dot = functools.partial(
        lax.dot_general, dimension_numbers=(dims, ((), ())), preferred_element_type=F32
    )
    return dot(lh, rh) + (dot(ll, rh) + dot(lh, rl))


def kernel(
    factor,
    vol_ref, up_ref, k_hbm, out_ref, vg_ref, kg_ref,
    k_f, pad_v, pad_u, col_v, col_u, halo_v, halo_u,
    wv_hi, wv_lo, wu_hi, wu_lo, vt_hi, vt_lo, acc_o, acc_g,
    part, pair, summed, r1, s2, r2, mid, q1, low, rz, fin, agz,
    z1, zmid, z2, zlow, z3,
    ksem, local_sem, send_sem, recv_sem,
):
    z, y, w = lax.axis_index("dev"), lax.axis_index("ha"), lax.axis_index("wa")
    core = lax.rem(w, 2)
    x = lax.div(w, 2)

    def step(i, by, n):
        return lax.rem(i + (by + n), n)

    counter = [0]
    sent = []

    def copy(src, dst, device):
        i = counter[0]
        counter[0] += 1
        return pltpu.make_async_remote_copy(
            src_ref=src, dst_ref=dst, send_sem=send_sem.at[i], recv_sem=recv_sem.at[i],
            device_id=device, device_id_type=MESH,
        )

    def start(*copies):
        for c in copies:
            c.start()
            sent.append(c)
        return copies

    peers = []
    for sd in (-1, 0, 1):
        for sh in (-1, 0, 1):
            if (sd, sh) != (0, 0):
                peers.append({"dev": step(z, sd, 8), "ha": step(y, sh, 4)})
    for k in range(2, 7):
        peers.append({"dev": step(z, k, 8)})
    for k in (-2, -1, 1, 2, 4):
        peers.append({"wa": step(w, k, 8)})
    peers.append({"ha": step(y, 2, 4)})
    barrier = pltpu.get_barrier_semaphore()
    for peer in peers:
        pl.semaphore_signal(barrier, inc=1, device_id=peer, device_id_type=MESH)
    load_u = pltpu.make_async_copy(up_ref, pad_u.at[pl.ds(1, 4), pl.ds(1, 8)], local_sem.at[0])
    load_v = pltpu.make_async_copy(vol_ref, pad_v.at[pl.ds(1, 4), pl.ds(1, 8)], local_sem.at[1])
    load_v.start()
    load_u.start()
    k_copies = [
        pltpu.make_async_copy(k_hbm.at[pl.ds(9 * i, 9)], k_f.at[pl.ds(9 * i, 9)], ksem.at[i])
        for i in range(3)
    ]
    for c in k_copies:
        c.start()
    acc_o[...] = jnp.zeros_like(acc_o)
    acc_g[...] = jnp.zeros_like(acc_g)
    pl.semaphore_wait(barrier, len(peers))

    def send_faces(src, pad):
        copies = []
        for sd in (-1, 0, 1):
            for sh in (-1, 0, 1):
                if (sd, sh) == (0, 0):
                    continue
                d_src, d_dst, d_n = ((0, 5, 1), (0, 1, 4), (3, 0, 1))[sd + 1]
                h_src, h_dst, h_n = ((0, 9, 1), (0, 1, 8), (7, 0, 1))[sh + 1]
                copies.append(copy(
                    src.at[pl.ds(d_src, d_n), pl.ds(h_src, h_n)],
                    pad.at[pl.ds(d_dst, d_n), pl.ds(h_dst, h_n)],
                    {"dev": step(z, sd, 8), "ha": step(y, sh, 4)},
                ))
        return start(*copies)

    def send_columns(pad, col, halo):
        col[0] = pad[:, :, 0:1, :]
        col[1] = pad[:, :, 7:8, :]
        return start(
            copy(col.at[0], halo.at[1], {"wa": step(w, -1, 8)}),
            copy(col.at[1], halo.at[0], {"wa": step(w, 1, 8)}),
        )

    def arrive(copies):
        for c in copies:
            c.wait_recv()

    def windows(pad, halo, hi_ref, lo_ref, shifts):
        def body(d, carry):
            rows = pl.ds(pl.multiple_of(d * 64, 64), 64)
            plane = pad[d]
            at = lax.broadcasted_iota(jnp.int32, plane.shape, 1)
            for c in shifts:
                shifted = plane
                if c != 1:
                    edge = jnp.broadcast_to(halo[c // 2, d], plane.shape)
                    by, row = ((1, 0), None, (7, 7))[c]
                    shifted = jnp.where(at == row, edge, pltpu.roll(plane, by, 1))
                for b in range(3):
                    hi, lo = split(shifted[b : b + 8].reshape(64, plane.shape[-1]))
                    hi_ref[3 * b + c, rows, :] = hi
                    lo_ref[3 * b + c, rows, :] = lo
            return carry

        lax.fori_loop(0, 6, body, 0)

    def window(hi_ref, lo_ref, t):
        rows = pl.ds(pl.multiple_of(lax.div(t, 9) * 64, 64), 256)
        i = lax.rem(t, 9)
        return hi_ref[i, rows, :], lo_ref[i, rows, :]

    def kernel_grad(g):
        def body(i, carry):
            upwin = window(wu_hi, wu_lo, 26 - tap(4 * g + i))
            res = dot3((vt_hi[...], vt_lo[...]), upwin, ((1,), (0,)))
            for block in range(8):
                for half in range(2):
                    part[g, block % 2, block // 2, 2 * i + half] = res[
                        32 * block : 32 * block + 32, 128 * half : 128 * half + 128
                    ]
            return carry

        taps = min(4, 27 - 4 * g)
        lax.fori_loop(0, taps, body, 0)
        for i in range(taps, 4):
            for j in (2 * i, 2 * i + 1):
                part[g, :, :, j] = jnp.zeros((2, 4, 32, 128), F32)
        groups[g].pair()

    def products(first, last):
        def body(t, carry):
            k = split(k_f[t])
            acc_o[...] += dot3(window(wv_hi, wv_lo, t), k, ((1,), (0,)))
            acc_g[...] += dot3(window(wu_hi, wu_lo, 26 - t), k, ((1,), (1,)))
            return carry

        lax.fori_loop(first, last, body, 0)

    def place(axis):
        return {"x": x, "y": y, "z": z}[axis]

    def away(axis, by):
        if axis == "x":
            return {"wa": step(w, 2 * by, 8)}
        return {"ha": step(y, by, 4)} if axis == "y" else {"dev": step(z, by, 8)}

    def direct(axis, chunk, recv):
        n = 8 if axis == "z" else 4
        return start(*(
            copy(chunk(step(place(axis), k, n)), recv.at[k - 1], away(axis, k)) for k in range(1, n)
        ))

    def direct_sum(axis, copies, chunk, recv):
        arrive(copies)
        total = chunk(place(axis))[...]
        for k in range(len(copies)):
            total = total + recv[k]
        return total

    def halves(ref, h):
        if len(ref.shape) == 4:
            return ref.at[:, pl.ds(4 * h, 4)]
        return ref.at[pl.ds(4 * h, 4)]

    def ring_1(axis, chunk, recv):
        far = chunk(step(place(axis), 2, 4))
        return start(
            copy(halves(far, 0), recv.at[0], away(axis, 1)),
            copy(halves(far, 1), recv.at[1], away(axis, -1)),
        )

    def ring_2(axis, copies, chunk, recv, stage, recv_2):
        arrive(copies)
        for h, by in ((0, 1), (1, -1)):
            near = chunk(step(place(axis), by, 4))
            halves(stage.at[h], h)[...] = halves(near, h)[...] + recv[h]
            halves(stage.at[h], 1 - h)[...] = halves(near, 1 - h)[...]
        return start(
            copy(stage.at[0], recv_2.at[0], away(axis, 1)),
            copy(stage.at[1], recv_2.at[1], away(axis, -1)),
        )

    def rows_of(ref, k):
        rows = pl.ds(pl.multiple_of(k * 8, 8), 8)
        return ref.at[(slice(None),) * (len(ref.shape) - 2) + (rows,)]

    class Group:
        def __init__(self, g):
            self.g = g
            self.slot = (g + GROUPS - 1) % GROUPS
            self.sum = summed.at[g]

        def pair(self):
            self.c = start(copy(part.at[self.g, 1 - core], pair.at[self.g], {"wa": w + 1 - 2 * core}))

        def add_pair(self):
            arrive(self.c)
            self.sum[...] = part[self.g, core] + pair[self.g]

    class PlaneGroup(Group):
        def __init__(self, g):
            super().__init__(g)
            self.first = FIRST[g]
            self.second = "y" if self.first == "x" else "x"
            n = FIRST[:g].count(self.first)
            i = 0 if self.first == "x" else 1
            self.r1, self.s2, self.r2 = r1[i].at[n], s2[i].at[n], r2[i].at[n]
            self.mid = mid[i].at[n]
            self.q1 = q1.at[self.slot]
            if self.first == "x":
                self.chunk_1 = lambda k: self.sum.at[k]
                self.chunk_2 = lambda k: rows_of(self.mid, k)
            else:
                self.chunk_1 = lambda k: rows_of(self.sum, k)
                self.chunk_2 = lambda k: self.mid.at[k]

        def e1(self):
            self.add_pair()
            self.c = ring_1(self.first, self.chunk_1, self.r1)

        def e2(self):
            self.c = ring_2(self.first, self.c, self.chunk_1, self.r1, self.s2, self.r2)

        def e3(self):
            self.mid[...] = direct_sum(self.first, self.c, self.chunk_1, self.r2)
            self.c = direct(self.second, self.chunk_2, self.q1)

        def e4(self):
            low[self.slot] = direct_sum(self.second, self.c, self.chunk_2, self.q1)

    class DepthGroup(Group):
        def __init__(self, g):
            super().__init__(g)
            self.chunk_1 = lambda k: self.sum.at[:, k]
            self.chunk_2 = lambda k: zmid.at[k]
            self.chunk_3 = lambda k: rows_of(zlow, k)

        def e1(self):
            self.add_pair()
            self.c = direct("z", self.chunk_1, z1)

        def e2(self):
            zmid[...] = direct_sum("z", self.c, self.chunk_1, z1)
            self.c = direct("x", self.chunk_2, z2)

        def e3(self):
            zlow[...] = direct_sum("x", self.c, self.chunk_2, z2)
            self.c = direct("y", self.chunk_3, z3)

        def result(self):
            return direct_sum("y", self.c, self.chunk_3, z3)

    class Batch:
        def __init__(self, i):
            self.i = i
            lo, hi = BATCHES[i]
            self.n = hi - lo - (1 if hi == GROUPS else 0)
            self.depth_group = hi == GROUPS
            self.lo = lo
            self.sums = pl.ds(lo, self.n)
            self.all = pl.ds(lo, hi - lo)

        def e6(self):
            self.c = start(*(
                copy(low.at[self.sums, step(z, k, 8)], rz.at[k - 1, self.sums], {"dev": step(z, k, 8)})
                for k in range(1, 8)
            ))

        def e7(self):
            arrive(self.c)
            total = low[self.sums, z]
            for k in range(7):
                total = total + rz[k, self.sums]
            fin[self.sums] = total * factor
            if self.depth_group:
                fin[GROUPS - 1] = groups[0].result() * factor
            agz_at = lambda k: agz.at[
                self.all, lax.div(k, 2), :, pl.ds(pl.multiple_of(lax.rem(k, 2) * 128, 128), 128)
            ]
            agz_at(z)[...] = fin[self.all]
            first = counter[0]
            start(*(copy(fin.at[self.all], agz_at(z), {"dev": step(z, k, 8)}) for k in range(1, 8)))
            self.c = [
                self.landed(first + k - 1, agz_at(step(z, -k, 8)), {"dev": step(z, k, 8)})
                for k in range(1, 8)
            ]

        def landed(self, i, slot, device):
            return pltpu.make_async_remote_copy(
                src_ref=slot, dst_ref=slot, send_sem=send_sem.at[i], recv_sem=recv_sem.at[i],
                device_id=device, device_id_type=MESH,
            )

        def e8(self):
            arrive(self.c)
            first = counter[0]
            here = agz.at[self.all]
            there = lambda k: rows_of(kg_ref.at[self.all], k)
            self.local = pltpu.make_async_copy(here, there(y), local_sem.at[4 + self.i])
            self.local.start()
            start(*(copy(here, there(y), {"ha": step(y, k, 4)}) for k in range(1, 4)))
            self.c = [
                self.landed(first + k - 1, there(step(y, -k, 4)), {"ha": step(y, k, 4)})
                for k in range(1, 4)
            ]

        def e9(self):
            self.local.wait()
            arrive(self.c)

    groups = [(DepthGroup if FIRST[g] == "z" else PlaneGroup)(g) for g in range(GROUPS)]
    batches = [Batch(i) for i in range(len(BATCHES))]

    faces_u = send_faces(up_ref, pad_u)
    load_v.wait()
    hi, lo = split(pad_v[1:5, 1:9].reshape(256, 256).T)
    vt_hi[...] = hi
    vt_lo[...] = lo
    load_u.wait()
    arrive(faces_u)
    cols_u = send_columns(pad_u, col_u, halo_u)
    faces_v = send_faces(vol_ref, pad_v)
    windows(pad_u, halo_u, wu_hi, wu_lo, (1,))
    kernel_grad(0)
    kernel_grad(1)
    groups[0].e1()
    arrive(cols_u)
    windows(pad_u, halo_u, wu_hi, wu_lo, (0, 2))
    groups[1].e1()
    kernel_grad(2)
    kernel_grad(3)
    groups[2].e1()
    arrive(faces_v)
    cols_v = send_columns(pad_v, col_v, halo_v)
    kernel_grad(4)
    groups[3].e1()
    groups[1].e2()
    kernel_grad(5)
    groups[4].e1()
    groups[2].e2()
    kernel_grad(6)
    groups[5].e1()
    groups[3].e2()
    windows(pad_v, halo_v, wv_hi, wv_lo, (1,))
    groups[6].e1()
    groups[4].e2()
    arrive(cols_v)
    windows(pad_v, halo_v, wv_hi, wv_lo, (0, 2))
    for c in k_copies:
        c.wait()
    groups[5].e2()
    products(0, 2)
    groups[6].e2()
    groups[1].e3()
    groups[2].e3()
    products(2, 7)
    groups[3].e3()
    groups[4].e3()
    products(7, 11)
    groups[1].e4()
    groups[2].e4()
    products(11, 14)
    groups[5].e3()
    groups[6].e3()
    groups[3].e4()
    groups[4].e4()
    batches[0].e6()
    products(14, 18)
    groups[0].e2()
    groups[5].e4()
    groups[6].e4()
    batches[1].e6()
    products(18, 22)
    batches[0].e7()
    groups[0].e3()
    products(22, 27)
    out_store = pltpu.make_async_copy(acc_o, out_ref, local_sem.at[2])
    vg_store = pltpu.make_async_copy(acc_g, vg_ref, local_sem.at[3])
    out_store.start()
    vg_store.start()
    batches[1].e7()
    batches[0].e8()
    batches[1].e8()
    batches[0].e9()
    batches[1].e9()
    out_store.wait()
    vg_store.wait()
    assert counter[0] == N_SEM, counter[0]
    for c in sent:
        c.wait_send()


def move(out_in, vg_in, kg_in, out_ref, vg_ref, kg_ref, out_v, vg_v, kg_v, sem, sem_2):
    ins = [
        pltpu.make_async_copy(src, dst, sem.at[i])
        for i, (src, dst) in enumerate(((out_in, out_v), (vg_in, vg_v), (kg_in, kg_v)))
    ]
    for c in ins:
        c.start()
    copies = [
        pltpu.make_async_copy(out_v, out_ref, sem_2.at[27]),
        pltpu.make_async_copy(vg_v, vg_ref, sem_2.at[28]),
    ]
    for c, then in zip(ins, copies):
        c.wait()
        then.start()
    ins[2].wait()
    for u in range(27):
        slot = (u // 4 + GROUPS - 1) % GROUPS
        copies.append(pltpu.make_async_copy(kg_v.at[slot, u % 4], kg_ref.at[tap(u)], sem_2.at[u]))
        copies[-1].start()
    for c in copies:
        c.wait()


def per_device(factor, volume, kernel_taps, upstream):
    nx, ny = FIRST.count("x"), FIRST.count("y")
    vmem = pltpu.VMEM
    scratch = [
        vmem((27, 256, 256), F32),
        vmem((6, 10, 8, 256), F32), vmem((6, 10, 8, 256), F32),
        vmem((2, 6, 10, 1, 256), F32), vmem((2, 6, 10, 1, 256), F32),
        vmem((2, 6, 10, 1, 256), F32), vmem((2, 6, 10, 1, 256), F32),
        vmem((9, 384, 256), BF16), vmem((9, 384, 256), BF16),
        vmem((9, 384, 256), BF16), vmem((9, 384, 256), BF16),
        vmem((256, 256), BF16), vmem((256, 256), BF16),
        vmem((256, 256), F32), vmem((256, 256), F32),
        vmem((GROUPS, 2, 4, 8, 32, 128), F32),
        vmem((GROUPS, 4, 8, 32, 128), F32),
        vmem((GROUPS, 4, 8, 32, 128), F32),
        [vmem((nx, 2, 4, 32, 128), F32), vmem((ny, 2, 4, 4, 8, 128), F32)],
        [vmem((nx, 2, 8, 32, 128), F32), vmem((ny, 2, 4, 8, 8, 128), F32)],
        [vmem((nx, 2, 8, 32, 128), F32), vmem((ny, 2, 4, 8, 8, 128), F32)],
        [vmem((nx, 8, 32, 128), F32), vmem((ny, 4, 8, 8, 128), F32)],
        vmem((GROUPS, 3, 8, 8, 128), F32),
        vmem((GROUPS, 8, 8, 128), F32),
        vmem((7, GROUPS, 8, 128), F32),
        vmem((GROUPS, 8, 128), F32),
        vmem((GROUPS, 4, 8, 256), F32),
        vmem((7, 4, 32, 128), F32), vmem((4, 32, 128), F32),
        vmem((3, 32, 128), F32), vmem((32, 128), F32),
        vmem((3, 8, 128), F32),
        pltpu.SemaphoreType.DMA((3,)),
        pltpu.SemaphoreType.DMA((4 + len(BATCHES),)),
        pltpu.SemaphoreType.DMA((N_SEM,)),
        pltpu.SemaphoreType.DMA((N_SEM,)),
    ]
    here = pl.BlockSpec(memory_space=pl.ANY)
    flat = jax.ShapeDtypeStruct((256, 256), F32)
    output, volume_grad, kg = pl.pallas_call(
        functools.partial(kernel, factor),
        out_shape=(flat, flat, jax.ShapeDtypeStruct((GROUPS, 4, 32, 256), F32)),
        in_specs=[here] * 3,
        out_specs=(here,) * 3,
        scratch_shapes=scratch,
        compiler_params=pltpu.CompilerParams(
            collective_id=0, has_side_effects=True, vmem_limit_bytes=56 * 2**20
        ),
    )(volume, upstream, jnp.transpose(kernel_taps, (1, 0, 2)))
    output, volume_grad, kg = pl.pallas_call(
        move,
        out_shape=(flat, flat, jax.ShapeDtypeStruct((27, 32, 256), F32)),
        in_specs=[here] * 3,
        out_specs=(here,) * 3,
        scratch_shapes=[
            vmem((256, 256), F32), vmem((256, 256), F32), vmem((GROUPS, 4, 32, 256), F32),
            pltpu.SemaphoreType.DMA((3,)), pltpu.SemaphoreType.DMA((29,)),
        ],
    )(output, volume_grad, kg)
    return (
        output.reshape(volume.shape),
        volume_grad.reshape(volume.shape),
        jnp.transpose(kg, (1, 0, 2)),
    )


def solution(mesh):
    cells = 256 * mesh.shape["dev"] * mesh.shape["ha"] * mesh.shape["wa"]
    place = P("dev", "ha", "wa", None)
    return jax.shard_map(
        functools.partial(per_device, 1.0 / math.sqrt(cells)),
        mesh=mesh,
        in_specs=(place, P(), place),
        out_specs=(place, place, P("wa", None, None)),
        check_vma=False,
    )
```

```python
import functools
import math

import jax
import jax.numpy as jnp
from jax import lax
from jax.experimental import pallas as pl
from jax.experimental.pallas import tpu as pltpu
from jax.sharding import PartitionSpec as P

MESH = pl.DeviceIdType.MESH
F32 = jnp.float32
BF16 = jnp.bfloat16

GROUPS = 7
FIRST = ("x", "y", "z", "x", "y", "x", "y")
DEPTH = FIRST.index("z")
SLOT = (0, 1, 6, 2, 3, 4, 5)
BATCHES = ((0, 2), (2, 4), (4, 7))
N_SEM = 2 * 26 + GROUPS + 6 * (2 + 2 + 3) + (7 + 3 + 3) + len(BATCHES) * (7 + 7 + 3)


def tap(u):
    if isinstance(u, int):
        return u + 9 if u < 9 else u - 9 if u < 18 else u
    return jnp.where(u < 9, u + 9, jnp.where(u < 18, u - 9, u))


def split(x):
    hi = x.astype(BF16)
    return hi, (x - hi.astype(F32)).astype(BF16)


def dot3(lhs, rhs, dims):
    (lh, ll), (rh, rl) = lhs, rhs
    dot = functools.partial(
        lax.dot_general, dimension_numbers=(dims, ((), ())), preferred_element_type=F32
    )
    return dot(lh, rh) + (dot(ll, rh) + dot(lh, rl))


def kernel(
    factor,
    vol_ref, up_ref, k_hbm, out_ref, vg_ref, kg_ref,
    k_f, pad_v, pad_u, col_v, col_u, halo_v, halo_u,
    wv_hi, wv_lo, wu_hi, wu_lo, vt_hi, vt_lo, acc_o, acc_g,
    part, pair, summed, r1, s2, r2, mid, q1, low, rz, fin, agz,
    z1, zmid, z2, zlow, z3,
    ksem, local_sem, send_sem, recv_sem,
):
    z, y, w = lax.axis_index("dev"), lax.axis_index("ha"), lax.axis_index("wa")
    core = lax.rem(w, 2)
    x = lax.div(w, 2)

    def step(i, by, n):
        return lax.rem(i + (by + n), n)

    counter = [0]
    sent = []

    def copy(src, dst, device):
        i = counter[0]
        counter[0] += 1
        return pltpu.make_async_remote_copy(
            src_ref=src, dst_ref=dst, send_sem=send_sem.at[i], recv_sem=recv_sem.at[i],
            device_id=device, device_id_type=MESH,
        )

    def start(*copies):
        for c in copies:
            c.start()
            sent.append(c)
        return copies

    around = [
        (sd, sh, sw) for sd in (0, -1, 1) for sh in (-1, 0, 1) for sw in (-1, 0, 1)
        if (sd, sh, sw) != (0, 0, 0)
    ]

    def neighbour(sd, sh, sw):
        return {"dev": step(z, sd, 8), "ha": step(y, sh, 4), "wa": step(w, sw, 8)}

    peers = [neighbour(*by) for by in around]
    for k in range(2, 7):
        peers.append({"dev": step(z, k, 8)})
    for k in (-2, 2, 4):
        peers.append({"wa": step(w, k, 8)})
    peers.append({"ha": step(y, 2, 4)})
    barrier = pltpu.get_barrier_semaphore()
    for peer in peers:
        pl.semaphore_signal(barrier, inc=1, device_id=peer, device_id_type=MESH)
    def cut_columns(pad, col):
        col[0] = pad[1:5, 1:9, 7:8, :]
        col[1] = pad[1:5, 1:9, 0:1, :]

    load_u = pltpu.make_async_copy(up_ref, pad_u.at[pl.ds(1, 4), pl.ds(1, 8)], local_sem.at[0])
    load_v = pltpu.make_async_copy(vol_ref, pad_v.at[pl.ds(1, 4), pl.ds(1, 8)], local_sem.at[1])
    load_u.start()
    load_v.start()
    k_copies = [
        pltpu.make_async_copy(k_hbm.at[pl.ds(9 * i, 9)], k_f.at[pl.ds(9 * i, 9)], ksem.at[i])
        for i in range(3)
    ]
    for c in k_copies:
        c.start()
    acc_o[...] = jnp.zeros_like(acc_o)
    acc_g[...] = jnp.zeros_like(acc_g)
    load_u.wait()
    cut_columns(pad_u, col_u)
    load_v.wait()
    cut_columns(pad_v, col_v)
    hi, lo = split(pad_v[1:5, 1:9].reshape(256, 256).T)
    vt_hi[...] = hi
    vt_lo[...] = lo
    pl.semaphore_wait(barrier, len(peers))

    def send_halo(src, pad, col, halo, pieces):
        copies = []
        for sd, sh, sw in pieces:
            d_src, d_dst, d_n = ((0, 5, 1), (0, 1, 4), (3, 0, 1))[sd + 1]
            h_src, h_dst, h_n = ((0, 9, 1), (0, 1, 8), (7, 0, 1))[sh + 1]
            at = (pl.ds(d_src, d_n), pl.ds(h_src, h_n))
            to = (pl.ds(d_dst, d_n), pl.ds(h_dst, h_n))
            if sw == 0:
                a, b = src.at[at], pad.at[to]
            else:
                side = 0 if sw == 1 else 1
                a, b = col.at[(side,) + at], halo.at[(side,) + to]
            copies.append(copy(a, b, neighbour(sd, sh, sw)))
        return start(*copies)

    def arrive(copies):
        for c in copies:
            c.wait_recv()

    def windows(pad, halo, hi_ref, lo_ref, planes):
        def body(i, carry):
            d = planes.start + i * planes.step
            rows = pl.ds(pl.multiple_of(d * 64, 64), 64)
            plane = pad[d]
            at = lax.broadcasted_iota(jnp.int32, plane.shape, 1)
            before = jnp.broadcast_to(halo[0, d], plane.shape)
            after = jnp.broadcast_to(halo[1, d], plane.shape)
            shifted = (
                jnp.where(at == 0, before, pltpu.roll(plane, 1, 1)),
                plane,
                jnp.where(at == 7, after, pltpu.roll(plane, 7, 1)),
            )
            for b in range(3):
                for c in range(3):
                    hi, lo = split(shifted[c][b : b + 8].reshape(64, plane.shape[-1]))
                    hi_ref[3 * b + c, rows, :] = hi
                    lo_ref[3 * b + c, rows, :] = lo
            return carry

        lax.fori_loop(0, len(planes), body, 0)

    def window(hi_ref, lo_ref, t):
        rows = pl.ds(pl.multiple_of(lax.div(t, 9) * 64, 64), 256)
        i = lax.rem(t, 9)
        return hi_ref[i, rows, :], lo_ref[i, rows, :]

    def kernel_grad(g):
        def body(i, carry):
            upwin = window(wu_hi, wu_lo, 26 - tap(4 * g + i))
            res = dot3((vt_hi[...], vt_lo[...]), upwin, ((1,), (0,)))
            for block in range(8):
                for half in range(2):
                    part[g, block % 2, block // 2, 2 * i + half] = res[
                        32 * block : 32 * block + 32, 128 * half : 128 * half + 128
                    ]
            return carry

        taps = min(4, 27 - 4 * g)
        lax.fori_loop(0, taps, body, 0)
        for i in range(taps, 4):
            for j in (2 * i, 2 * i + 1):
                part[g, :, :, j] = jnp.zeros((2, 4, 32, 128), F32)
        groups[g].pair()

    def products(first, last):
        def body(t, carry):
            k = split(k_f[t])
            acc_o[...] += dot3(window(wv_hi, wv_lo, t), k, ((1,), (0,)))
            acc_g[...] += dot3(window(wu_hi, wu_lo, 26 - t), k, ((1,), (1,)))
            return carry

        lax.fori_loop(first, last, body, 0)

    def place(axis):
        return {"x": x, "y": y, "z": z}[axis]

    def away(axis, by):
        if axis == "x":
            return {"wa": step(w, 2 * by, 8)}
        return {"ha": step(y, by, 4)} if axis == "y" else {"dev": step(z, by, 8)}

    def direct(axis, chunk, recv):
        n = 8 if axis == "z" else 4
        return start(*(
            copy(chunk(step(place(axis), k, n)), recv.at[k - 1], away(axis, k)) for k in range(1, n)
        ))

    def direct_sum(axis, copies, chunk, recv):
        arrive(copies)
        total = chunk(place(axis))[...]
        for k in range(len(copies)):
            total = total + recv[k]
        return total

    def halves(ref, h):
        if len(ref.shape) == 4:
            return ref.at[:, pl.ds(4 * h, 4)]
        return ref.at[pl.ds(4 * h, 4)]

    def ring_1(axis, chunk, recv):
        far = chunk(step(place(axis), 2, 4))
        return start(
            copy(halves(far, 0), recv.at[0], away(axis, 1)),
            copy(halves(far, 1), recv.at[1], away(axis, -1)),
        )

    def ring_2(axis, copies, chunk, recv, stage, recv_2):
        arrive(copies)
        for h, by in ((0, 1), (1, -1)):
            near = chunk(step(place(axis), by, 4))
            halves(stage.at[h], h)[...] = halves(near, h)[...] + recv[h]
            halves(stage.at[h], 1 - h)[...] = halves(near, 1 - h)[...]
        return start(
            copy(stage.at[0], recv_2.at[0], away(axis, 1)),
            copy(stage.at[1], recv_2.at[1], away(axis, -1)),
        )

    def rows_of(ref, k):
        rows = pl.ds(pl.multiple_of(k * 8, 8), 8)
        return ref.at[(slice(None),) * (len(ref.shape) - 2) + (rows,)]

    class Group:
        def __init__(self, g):
            self.g = g
            self.slot = SLOT[g]
            self.sum = summed.at[g]

        def pair(self):
            self.c = start(copy(part.at[self.g, 1 - core], pair.at[self.g], {"wa": w + 1 - 2 * core}))

        def add_pair(self):
            arrive(self.c)
            self.sum[...] = part[self.g, core] + pair[self.g]

    class PlaneGroup(Group):
        def __init__(self, g):
            super().__init__(g)
            self.first = FIRST[g]
            self.second = "y" if self.first == "x" else "x"
            n = FIRST[:g].count(self.first)
            i = 0 if self.first == "x" else 1
            self.r1, self.s2, self.r2 = r1[i].at[n], s2[i].at[n], r2[i].at[n]
            self.mid = mid[i].at[n]
            self.q1 = q1.at[self.slot]
            if self.first == "x":
                self.chunk_1 = lambda k: self.sum.at[k]
                self.chunk_2 = lambda k: rows_of(self.mid, k)
            else:
                self.chunk_1 = lambda k: rows_of(self.sum, k)
                self.chunk_2 = lambda k: self.mid.at[k]

        def e1(self):
            self.add_pair()
            self.c = ring_1(self.first, self.chunk_1, self.r1)

        def e2(self):
            self.c = ring_2(self.first, self.c, self.chunk_1, self.r1, self.s2, self.r2)

        def e3(self):
            self.mid[...] = direct_sum(self.first, self.c, self.chunk_1, self.r2)
            self.c = direct(self.second, self.chunk_2, self.q1)

        def e4(self):
            low[self.slot] = direct_sum(self.second, self.c, self.chunk_2, self.q1)

    class DepthGroup(Group):
        def __init__(self, g):
            super().__init__(g)
            self.chunk_1 = lambda k: self.sum.at[:, k]
            self.chunk_2 = lambda k: zmid.at[k]
            self.chunk_3 = lambda k: rows_of(zlow, k)

        def e1(self):
            self.add_pair()
            self.c = direct("z", self.chunk_1, z1)

        def e2(self):
            zmid[...] = direct_sum("z", self.c, self.chunk_1, z1)
            self.c = direct("x", self.chunk_2, z2)

        def e3(self):
            zlow[...] = direct_sum("x", self.c, self.chunk_2, z2)
            self.c = direct("y", self.chunk_3, z3)

        def result(self):
            return direct_sum("y", self.c, self.chunk_3, z3)

    class Batch:
        def __init__(self, i):
            self.i = i
            lo, hi = BATCHES[i]
            self.n = hi - lo - (1 if hi == GROUPS else 0)
            self.depth_group = hi == GROUPS
            self.lo = lo
            self.sums = pl.ds(lo, self.n)
            self.all = pl.ds(lo, hi - lo)

        def e6(self):
            self.c = start(*(
                copy(low.at[self.sums, step(z, k, 8)], rz.at[k - 1, self.sums], {"dev": step(z, k, 8)})
                for k in range(1, 8)
            ))

        def e7(self):
            arrive(self.c)
            total = low[self.sums, z]
            for k in range(7):
                total = total + rz[k, self.sums]
            fin[self.sums] = total * factor
            if self.depth_group:
                fin[GROUPS - 1] = groups[DEPTH].result() * factor
            agz_at = lambda k: agz.at[
                self.all, lax.div(k, 2), :, pl.ds(pl.multiple_of(lax.rem(k, 2) * 128, 128), 128)
            ]
            agz_at(z)[...] = fin[self.all]
            first = counter[0]
            start(*(copy(fin.at[self.all], agz_at(z), {"dev": step(z, k, 8)}) for k in range(1, 8)))
            self.c = [
                self.landed(first + k - 1, agz_at(step(z, -k, 8)), {"dev": step(z, k, 8)})
                for k in range(1, 8)
            ]

        def landed(self, i, slot, device):
            return pltpu.make_async_remote_copy(
                src_ref=slot, dst_ref=slot, send_sem=send_sem.at[i], recv_sem=recv_sem.at[i],
                device_id=device, device_id_type=MESH,
            )

        def e8(self):
            arrive(self.c)
            first = counter[0]
            here = agz.at[self.all]
            there = lambda k: rows_of(kg_ref.at[self.all], k)
            self.local = pltpu.make_async_copy(here, there(y), local_sem.at[4 + self.i])
            self.local.start()
            start(*(copy(here, there(y), {"ha": step(y, k, 4)}) for k in range(1, 4)))
            self.c = [
                self.landed(first + k - 1, there(step(y, -k, 4)), {"ha": step(y, k, 4)})
                for k in range(1, 4)
            ]

        def e9(self):
            self.local.wait()
            arrive(self.c)

    groups = [(DepthGroup if FIRST[g] == "z" else PlaneGroup)(g) for g in range(GROUPS)]
    batches = [Batch(i) for i in range(len(BATCHES))]

    flat_u = send_halo(up_ref, pad_u, col_u, halo_u, around[:8])
    deep_u = send_halo(up_ref, pad_u, col_u, halo_u, around[8:])
    arrive(flat_u)
    windows(pad_u, halo_u, wu_hi, wu_lo, range(1, 5))
    kernel_grad(0)
    kernel_grad(1)
    arrive(deep_u)
    windows(pad_u, halo_u, wu_hi, wu_lo, range(0, 6, 5))
    groups[0].e1()
    kernel_grad(2)
    groups[1].e1()
    halos_v = send_halo(vol_ref, pad_v, col_v, halo_v, around)
    kernel_grad(3)
    groups[2].e1()
    kernel_grad(4)
    groups[3].e1()
    groups[0].e2()
    kernel_grad(5)
    groups[4].e1()
    groups[1].e2()
    kernel_grad(6)
    groups[5].e1()
    groups[3].e2()
    groups[6].e1()
    groups[4].e2()
    arrive(halos_v)
    windows(pad_v, halo_v, wv_hi, wv_lo, range(6))
    for c in k_copies:
        c.wait()
    groups[5].e2()
    groups[6].e2()
    products(0, 1)
    groups[0].e3()
    groups[1].e3()
    products(1, 6)
    groups[3].e3()
    groups[4].e3()
    groups[0].e4()
    groups[1].e4()
    batches[0].e6()
    products(6, 11)
    groups[5].e3()
    groups[6].e3()
    groups[3].e4()
    groups[4].e4()
    batches[1].e6()
    products(11, 16)
    groups[2].e2()
    batches[0].e7()
    groups[5].e4()
    groups[6].e4()
    batches[2].e6()
    products(16, 22)
    groups[2].e3()
    batches[1].e7()
    batches[0].e8()
    products(22, 27)
    out_store = pltpu.make_async_copy(acc_o, out_ref, local_sem.at[2])
    vg_store = pltpu.make_async_copy(acc_g, vg_ref, local_sem.at[3])
    out_store.start()
    vg_store.start()
    batches[2].e7()
    batches[1].e8()
    batches[2].e8()
    for batch in batches:
        batch.e9()
    out_store.wait()
    vg_store.wait()
    assert counter[0] == N_SEM, counter[0]
    for c in sent:
        c.wait_send()


def move(out_in, vg_in, kg_in, out_ref, vg_ref, kg_ref, out_v, vg_v, kg_v, sem, sem_2):
    ins = [
        pltpu.make_async_copy(src, dst, sem.at[i])
        for i, (src, dst) in enumerate(((out_in, out_v), (vg_in, vg_v), (kg_in, kg_v)))
    ]
    for c in ins:
        c.start()
    copies = [
        pltpu.make_async_copy(out_v, out_ref, sem_2.at[27]),
        pltpu.make_async_copy(vg_v, vg_ref, sem_2.at[28]),
    ]
    for c, then in zip(ins, copies):
        c.wait()
        then.start()
    ins[2].wait()
    for u in range(27):
        slot = SLOT[u // 4]
        copies.append(pltpu.make_async_copy(kg_v.at[slot, u % 4], kg_ref.at[tap(u)], sem_2.at[u]))
        copies[-1].start()
    for c in copies:
        c.wait()


def per_device(factor, volume, kernel_taps, upstream):
    nx, ny = FIRST.count("x"), FIRST.count("y")
    vmem = pltpu.VMEM
    scratch = [
        vmem((27, 256, 256), F32),
        vmem((6, 10, 8, 256), F32), vmem((6, 10, 8, 256), F32),
        vmem((2, 4, 8, 1, 256), F32), vmem((2, 4, 8, 1, 256), F32),
        vmem((2, 6, 10, 1, 256), F32), vmem((2, 6, 10, 1, 256), F32),
        vmem((9, 384, 256), BF16), vmem((9, 384, 256), BF16),
        vmem((9, 384, 256), BF16), vmem((9, 384, 256), BF16),
        vmem((256, 256), BF16), vmem((256, 256), BF16),
        vmem((256, 256), F32), vmem((256, 256), F32),
        vmem((GROUPS, 2, 4, 8, 32, 128), F32),
        vmem((GROUPS, 4, 8, 32, 128), F32),
        vmem((GROUPS, 4, 8, 32, 128), F32),
        [vmem((nx, 2, 4, 32, 128), F32), vmem((ny, 2, 4, 4, 8, 128), F32)],
        [vmem((nx, 2, 8, 32, 128), F32), vmem((ny, 2, 4, 8, 8, 128), F32)],
        [vmem((nx, 2, 8, 32, 128), F32), vmem((ny, 2, 4, 8, 8, 128), F32)],
        [vmem((nx, 8, 32, 128), F32), vmem((ny, 4, 8, 8, 128), F32)],
        vmem((GROUPS, 3, 8, 8, 128), F32),
        vmem((GROUPS, 8, 8, 128), F32),
        vmem((7, GROUPS, 8, 128), F32),
        vmem((GROUPS, 8, 128), F32),
        vmem((GROUPS, 4, 8, 256), F32),
        vmem((7, 4, 32, 128), F32), vmem((4, 32, 128), F32),
        vmem((3, 32, 128), F32), vmem((32, 128), F32),
        vmem((3, 8, 128), F32),
        pltpu.SemaphoreType.DMA((3,)),
        pltpu.SemaphoreType.DMA((4 + len(BATCHES),)),
        pltpu.SemaphoreType.DMA((N_SEM,)),
        pltpu.SemaphoreType.DMA((N_SEM,)),
    ]
    here = pl.BlockSpec(memory_space=pl.ANY)
    flat = jax.ShapeDtypeStruct((256, 256), F32)
    output, volume_grad, kg = pl.pallas_call(
        functools.partial(kernel, factor),
        out_shape=(flat, flat, jax.ShapeDtypeStruct((GROUPS, 4, 32, 256), F32)),
        in_specs=[here] * 3,
        out_specs=(here,) * 3,
        scratch_shapes=scratch,
        compiler_params=pltpu.CompilerParams(
            collective_id=0, has_side_effects=True, vmem_limit_bytes=56 * 2**20
        ),
    )(volume, upstream, jnp.transpose(kernel_taps, (1, 0, 2)))
    output, volume_grad, kg = pl.pallas_call(
        move,
        out_shape=(flat, flat, jax.ShapeDtypeStruct((27, 32, 256), F32)),
        in_specs=[here] * 3,
        out_specs=(here,) * 3,
        scratch_shapes=[
            vmem((256, 256), F32), vmem((256, 256), F32), vmem((GROUPS, 4, 32, 256), F32),
            pltpu.SemaphoreType.DMA((3,)), pltpu.SemaphoreType.DMA((29,)),
        ],
    )(output, volume_grad, kg)
    return (
        output.reshape(volume.shape),
        volume_grad.reshape(volume.shape),
        jnp.transpose(kg, (1, 0, 2)),
    )


def solution(mesh):
    cells = 256 * mesh.shape["dev"] * mesh.shape["ha"] * mesh.shape["wa"]
    place = P("dev", "ha", "wa", None)
    return jax.shard_map(
        functools.partial(per_device, 1.0 / math.sqrt(cells)),
        mesh=mesh,
        in_specs=(place, P(), place),
        out_specs=(place, place, P("wa", None, None)),
        check_vma=False,
    )
```

```python
import functools
import math

import jax
import jax.numpy as jnp
from jax import lax
from jax.experimental import pallas as pl
from jax.experimental.pallas import tpu as pltpu
from jax.sharding import PartitionSpec as P

MESH = pl.DeviceIdType.MESH
F32 = jnp.float32
BF16 = jnp.bfloat16

GROUPS = 7
FIRST = ("x", "y", "z", "x", "y", "x", "y")
DEPTH = FIRST.index("z")
SLOT = (0, 1, 4, 2, 3, 5, 6)
BATCHES = ((0, 2), (2, 5), (5, 7))
N_SEM = 2 * 26 + GROUPS + 6 * (4 + 2 + 3) + (7 + 3 + 3) + len(BATCHES) * (7 + 7 + 3)


def tap(u):
    return u + 9 if u < 9 else u - 9 if u < 18 else u


def split(x):
    hi = x.astype(BF16)
    return hi, (x - hi.astype(F32)).astype(BF16)


def dot3(lhs, rhs, dims):
    (lh, ll), (rh, rl) = lhs, rhs
    dot = functools.partial(
        lax.dot_general, dimension_numbers=(dims, ((), ())), preferred_element_type=F32
    )
    return dot(lh, rh) + (dot(ll, rh) + dot(lh, rl))


def kernel(
    factor,
    vol_ref, up_ref, k_hbm, out_ref, vg_ref, kg_ref,
    k_f, pad_v, pad_u, col_v, col_u, halo_v, halo_u,
    wv_hi, wv_lo, wu_hi, wu_lo, vt_hi, vt_lo,
    part, pair, summed, r1, s2, r2, mid, q1, low, rz, fin, agz, gathered,
    z1, zmid, z2, zlow, z3,
    ksem, local_sem, send_sem, recv_sem,
):
    z, y, w = lax.axis_index("dev"), lax.axis_index("ha"), lax.axis_index("wa")
    core = lax.rem(w, 2)
    x = lax.div(w, 2)

    def step(i, by, n):
        return lax.rem(i + (by + n), n)

    counter = [0]
    sent = []

    def copy(src, dst, device):
        i = counter[0]
        counter[0] += 1
        return pltpu.make_async_remote_copy(
            src_ref=src, dst_ref=dst, send_sem=send_sem.at[i], recv_sem=recv_sem.at[i],
            device_id=device, device_id_type=MESH,
        )

    def start(*copies):
        for c in copies:
            c.start()
            sent.append(c)
        return copies

    load_u = pltpu.make_async_copy(up_ref, pad_u.at[pl.ds(1, 4), pl.ds(1, 8)], local_sem.at[0])
    load_v = pltpu.make_async_copy(vol_ref, pad_v.at[pl.ds(1, 4), pl.ds(1, 8)], local_sem.at[1])
    load_u.start()
    load_v.start()
    around = [
        (sd, sh, sw) for sd in (0, -1, 1) for sh in (-1, 0, 1) for sw in (-1, 0, 1)
        if (sd, sh, sw) != (0, 0, 0)
    ]

    def neighbour(sd, sh, sw):
        return {"dev": step(z, sd, 8), "ha": step(y, sh, 4), "wa": step(w, sw, 8)}

    peers = [neighbour(*by) for by in around]
    for k in range(2, 7):
        peers.append({"dev": step(z, k, 8)})
    for k in (-2, 2, 4):
        peers.append({"wa": step(w, k, 8)})
    peers.append({"ha": step(y, 2, 4)})
    barrier = pltpu.get_barrier_semaphore()
    for peer in peers:
        pl.semaphore_signal(barrier, inc=1, device_id=peer, device_id_type=MESH)
    def cut_columns(pad, col):
        col[0] = pad[1:5, 1:9, 7:8, :]
        col[1] = pad[1:5, 1:9, 0:1, :]

    k_copies = [
        pltpu.make_async_copy(k_hbm.at[pl.ds(9 * i, 9)], k_f.at[pl.ds(9 * i, 9)], ksem.at[i])
        for i in range(3)
    ]
    pl.semaphore_wait(barrier, len(peers))

    def send_halo(src, pad, col, halo, pieces):
        copies = []
        for sd, sh, sw in pieces:
            d_src, d_dst, d_n = ((0, 5, 1), (0, 1, 4), (3, 0, 1))[sd + 1]
            h_src, h_dst, h_n = ((0, 9, 1), (0, 1, 8), (7, 0, 1))[sh + 1]
            at = (pl.ds(d_src, d_n), pl.ds(h_src, h_n))
            to = (pl.ds(d_dst, d_n), pl.ds(h_dst, h_n))
            if sw == 0:
                a, b = src.at[at], pad.at[to]
            else:
                side = 0 if sw == 1 else 1
                a, b = col.at[(side,) + at], halo.at[(side,) + to]
            copies.append(copy(a, b, neighbour(sd, sh, sw)))
        return start(*copies)

    def arrive(copies):
        for c in copies:
            c.wait_recv()

    def windows(pad, halo, hi_ref, lo_ref, planes):
        def body(i, carry):
            d = planes.start + i * planes.step
            rows = pl.ds(pl.multiple_of(d * 64, 64), 64)
            plane = pad[d]
            at = lax.broadcasted_iota(jnp.int32, plane.shape, 1)
            before = jnp.broadcast_to(halo[0, d], plane.shape)
            after = jnp.broadcast_to(halo[1, d], plane.shape)
            shifted = (
                jnp.where(at == 0, before, pltpu.roll(plane, 1, 1)),
                plane,
                jnp.where(at == 7, after, pltpu.roll(plane, 7, 1)),
            )
            for b in range(3):
                for c in range(3):
                    hi, lo = split(shifted[c][b : b + 8].reshape(64, plane.shape[-1]))
                    hi_ref[3 * b + c, rows, :] = hi
                    lo_ref[3 * b + c, rows, :] = lo
            return carry

        lax.fori_loop(0, len(planes), body, 0)

    def window(hi_ref, lo_ref, t):
        t = jnp.int32(t)
        rows = pl.ds(pl.multiple_of(lax.div(t, 9) * 64, 64), 256)
        i = lax.rem(t, 9)
        return hi_ref[i, rows, :], lo_ref[i, rows, :]

    def kernel_grad(g):
        taps = min(4, 27 - 4 * g)
        for i in range(taps):
            d, at = divmod(26 - tap(4 * g + i), 9)
            rows = slice(64 * d, 64 * d + 256)
            upwin = wu_hi[at, rows, :], wu_lo[at, rows, :]
            res = dot3((vt_hi[...], vt_lo[...]), upwin, ((1,), (0,)))
            for block in range(8):
                for half in range(2):
                    part[g, block % 2, block // 2, 2 * i + half] = res[
                        32 * block : 32 * block + 32, 128 * half : 128 * half + 128
                    ]
        for i in range(taps, 4):
            for j in (2 * i, 2 * i + 1):
                part[g, :, :, j] = jnp.zeros((2, 4, 32, 128), F32)
        groups[g].pair()

    def products(first, last):
        def add(taps):
            out, grad = 0.0, 0.0
            for t in taps:
                k = split(k_f[t])
                out += dot3(window(wv_hi, wv_lo, t), k, ((1,), (0,)))
                grad += dot3(window(wu_hi, wu_lo, 26 - t), k, ((1,), (1,)))
            out_ref[...] += out
            vg_ref[...] += grad

        def body(i, carry):
            add((first + 2 * i, first + 2 * i + 1))
            return carry

        lax.fori_loop(0, (last - first) // 2, body, 0)
        if (last - first) % 2:
            add((last - 1,))

    def place(axis):
        return {"x": x, "y": y, "z": z}[axis]

    def away(axis, by):
        if axis == "x":
            return {"wa": step(w, 2 * by, 8)}
        return {"ha": step(y, by, 4)} if axis == "y" else {"dev": step(z, by, 8)}

    def direct(axis, chunk, recv):
        n = 8 if axis == "z" else 4
        return start(*(
            copy(chunk(step(place(axis), k, n)), recv.at[k - 1], away(axis, k)) for k in range(1, n)
        ))

    def direct_sum(axis, copies, chunk, recv):
        arrive(copies)
        total = chunk(place(axis))[...]
        for k in range(len(copies)):
            total = total + recv[k]
        return total

    def halves(ref, h):
        if len(ref.shape) == 4:
            return ref.at[:, pl.ds(4 * h, 4)]
        return ref.at[pl.ds(4 * h, 4)]

    def ring_1(axis, chunk, recv, recv_2):
        i = place(axis)
        far, above, below = (chunk(step(i, k, 4)) for k in (2, 1, -1))
        return start(
            copy(halves(far, 0), recv.at[0], away(axis, 1)),
            copy(halves(far, 1), recv.at[1], away(axis, -1)),
        ), start(
            copy(halves(above, 1), halves(recv_2.at[0], 1), away(axis, 1)),
            copy(halves(below, 0), halves(recv_2.at[1], 0), away(axis, -1)),
        )

    def ring_2(axis, copies, chunk, recv, stage, recv_2):
        arrive(copies)
        for h, by in ((0, 1), (1, -1)):
            stage[h] = halves(chunk(step(place(axis), by, 4)), h)[...] + recv[h]
        return start(
            copy(stage.at[0], halves(recv_2.at[0], 0), away(axis, 1)),
            copy(stage.at[1], halves(recv_2.at[1], 1), away(axis, -1)),
        )

    def rows_of(ref, k):
        rows = pl.ds(pl.multiple_of(k * 8, 8), 8)
        return ref.at[(slice(None),) * (len(ref.shape) - 2) + (rows,)]

    class Group:
        def __init__(self, g):
            self.g = g
            self.slot = SLOT[g]
            self.sum = summed.at[g]

        def pair(self):
            self.c = start(copy(part.at[self.g, 1 - core], pair.at[self.g], {"wa": w + 1 - 2 * core}))

        def add_pair(self):
            arrive(self.c)
            self.sum[...] = part[self.g, core] + pair[self.g]

    class PlaneGroup(Group):
        def __init__(self, g):
            super().__init__(g)
            self.first = FIRST[g]
            self.second = "y" if self.first == "x" else "x"
            n = FIRST[:g].count(self.first)
            i = 0 if self.first == "x" else 1
            self.r1, self.s2, self.r2 = r1[i].at[n], s2[i].at[n], r2[i].at[n]
            self.mid = mid[i].at[n]
            self.q1 = q1.at[self.slot]
            if self.first == "x":
                self.chunk_1 = lambda k: self.sum.at[k]
                self.chunk_2 = lambda k: rows_of(self.mid, k)
            else:
                self.chunk_1 = lambda k: rows_of(self.sum, k)
                self.chunk_2 = lambda k: self.mid.at[k]

        def e1(self):
            self.add_pair()
            self.c, self.near = ring_1(self.first, self.chunk_1, self.r1, self.r2)

        def e2(self):
            self.c = ring_2(self.first, self.c, self.chunk_1, self.r1, self.s2, self.r2)

        def e3(self):
            arrive(self.near)
            self.mid[...] = direct_sum(self.first, self.c, self.chunk_1, self.r2)
            self.c = direct(self.second, self.chunk_2, self.q1)

        def e4(self):
            low[self.slot] = direct_sum(self.second, self.c, self.chunk_2, self.q1)

    class DepthGroup(Group):
        def __init__(self, g):
            super().__init__(g)
            self.chunk_1 = lambda k: self.sum.at[:, k]
            self.chunk_2 = lambda k: zmid.at[k]
            self.chunk_3 = lambda k: rows_of(zlow, k)

        def e1(self):
            self.add_pair()
            self.c = direct("z", self.chunk_1, z1)

        def e2(self):
            zmid[...] = direct_sum("z", self.c, self.chunk_1, z1)
            self.c = direct("x", self.chunk_2, z2)

        def e3(self):
            zlow[...] = direct_sum("x", self.c, self.chunk_2, z2)
            self.c = direct("y", self.chunk_3, z3)

        def result(self):
            return direct_sum("y", self.c, self.chunk_3, z3)

    class Batch:
        def __init__(self, i):
            self.i = i
            lo, hi = BATCHES[i]
            self.depth_group = hi == SLOT[DEPTH] + 1
            self.n = hi - lo - (1 if self.depth_group else 0)
            self.lo = lo
            self.sums = pl.ds(lo, self.n)
            self.all = pl.ds(lo, hi - lo)

        def e6(self):
            self.c = start(*(
                copy(low.at[self.sums, step(z, k, 8)], rz.at[k - 1, self.sums], {"dev": step(z, k, 8)})
                for k in range(1, 8)
            ))

        def e7(self):
            arrive(self.c)
            total = low[self.sums, z]
            for k in range(7):
                total = total + rz[k, self.sums]
            fin[self.sums] = total * factor
            if self.depth_group:
                fin[SLOT[DEPTH]] = groups[DEPTH].result() * factor
            agz_at = lambda k: agz.at[
                self.all, lax.div(k, 2), :, pl.ds(pl.multiple_of(lax.rem(k, 2) * 128, 128), 128)
            ]
            agz_at(z)[...] = fin[self.all]
            first = counter[0]
            start(*(copy(fin.at[self.all], agz_at(z), {"dev": step(z, k, 8)}) for k in range(1, 8)))
            self.c = [
                self.landed(first + k - 1, agz_at(step(z, -k, 8)), {"dev": step(z, k, 8)})
                for k in range(1, 8)
            ]

        def landed(self, i, slot, device):
            return pltpu.make_async_remote_copy(
                src_ref=slot, dst_ref=slot, send_sem=send_sem.at[i], recv_sem=recv_sem.at[i],
                device_id=device, device_id_type=MESH,
            )

        def e8(self):
            arrive(self.c)
            first = counter[0]
            here = agz.at[self.all]
            there = lambda k: rows_of(gathered.at[self.all], k)
            there(y)[...] = agz[self.all]
            start(*(copy(here, there(y), {"ha": step(y, k, 4)}) for k in range(1, 4)))
            self.c = [
                self.landed(first + k - 1, there(step(y, -k, 4)), {"ha": step(y, k, 4)})
                for k in range(1, 4)
            ]

        def e9(self):
            arrive(self.c)
            for u in range(27):
                if BATCHES[self.i][0] <= SLOT[u // 4] < BATCHES[self.i][1]:
                    kg_ref[tap(u)] = gathered[SLOT[u // 4], u % 4]

    groups = [(DepthGroup if FIRST[g] == "z" else PlaneGroup)(g) for g in range(GROUPS)]
    batches = [Batch(i) for i in range(len(BATCHES))]

    inner = [by for by in around if by[2] == 0]
    outer = [by for by in around if by[2] != 0]
    flat_u = send_halo(up_ref, pad_u, col_u, halo_u, inner[:2])
    deep_u = send_halo(up_ref, pad_u, col_u, halo_u, inner[2:])
    load_u.wait()
    cut_columns(pad_u, col_u)
    flat_u += send_halo(up_ref, pad_u, col_u, halo_u, outer[:6])
    deep_u += send_halo(up_ref, pad_u, col_u, halo_u, outer[6:])
    for c in k_copies:
        c.start()
    load_v.wait()
    cut_columns(pad_v, col_v)
    hi, lo = split(pad_v[1:5, 1:9].reshape(256, 256).T)
    vt_hi[...] = hi
    vt_lo[...] = lo
    out_ref[...] = jnp.zeros_like(out_ref)
    vg_ref[...] = jnp.zeros_like(vg_ref)
    arrive(flat_u)
    halos_v = send_halo(vol_ref, pad_v, col_v, halo_v, around)
    windows(pad_u, halo_u, wu_hi, wu_lo, range(1, 5))
    kernel_grad(0)
    kernel_grad(1)
    arrive(deep_u)
    windows(pad_u, halo_u, wu_hi, wu_lo, range(0, 6, 5))
    kernel_grad(2)
    groups[0].e1()
    kernel_grad(3)
    groups[1].e1()
    kernel_grad(4)
    groups[2].e1()
    groups[3].e1()
    kernel_grad(5)
    groups[4].e1()
    kernel_grad(6)
    groups[5].e1()
    groups[6].e1()
    groups[0].e2()
    groups[1].e2()
    groups[3].e2()
    groups[4].e2()
    arrive(halos_v)
    windows(pad_v, halo_v, wv_hi, wv_lo, range(6))
    groups[5].e2()
    groups[6].e2()
    for c in k_copies:
        c.wait()
    products(0, 8)
    groups[0].e3()
    groups[1].e3()
    products(8, 14)
    groups[3].e3()
    groups[4].e3()
    products(14, 18)
    groups[0].e4()
    groups[1].e4()
    batches[0].e6()
    products(18, 22)
    groups[5].e3()
    groups[6].e3()
    groups[2].e2()
    products(22, 24)
    groups[3].e4()
    groups[4].e4()
    batches[1].e6()
    products(24, 27)
    groups[2].e3()
    batches[0].e7()
    groups[5].e4()
    groups[6].e4()
    batches[2].e6()
    batches[1].e7()
    batches[0].e8()
    batches[2].e7()
    batches[1].e8()
    batches[2].e8()
    for batch in batches:
        batch.e9()
    assert counter[0] == N_SEM, counter[0]
    for c in sent:
        c.wait_send()


def store(out_in, vg_in, kg_in, out_ref, vg_ref, kg_ref, sem):
    copies = [
        pltpu.make_async_copy(src, dst, sem.at[i])
        for i, (src, dst) in enumerate(((kg_in, kg_ref), (out_in, out_ref), (vg_in, vg_ref)))
    ]
    for c in copies:
        c.start()
    for c in copies:
        c.wait()


def per_device(factor, volume, kernel_taps, upstream):
    nx, ny = FIRST.count("x"), FIRST.count("y")
    vmem = pltpu.VMEM
    scratch = [
        vmem((27, 256, 256), F32),
        vmem((6, 10, 8, 256), F32), vmem((6, 10, 8, 256), F32),
        vmem((2, 4, 8, 1, 256), F32), vmem((2, 4, 8, 1, 256), F32),
        vmem((2, 6, 10, 1, 256), F32), vmem((2, 6, 10, 1, 256), F32),
        vmem((9, 384, 256), BF16), vmem((9, 384, 256), BF16),
        vmem((9, 384, 256), BF16), vmem((9, 384, 256), BF16),
        vmem((256, 256), BF16), vmem((256, 256), BF16),
        vmem((GROUPS, 2, 4, 8, 32, 128), F32),
        vmem((GROUPS, 4, 8, 32, 128), F32),
        vmem((GROUPS, 4, 8, 32, 128), F32),
        [vmem((nx, 2, 4, 32, 128), F32), vmem((ny, 2, 4, 4, 8, 128), F32)],
        [vmem((nx, 2, 4, 32, 128), F32), vmem((ny, 2, 4, 4, 8, 128), F32)],
        [vmem((nx, 2, 8, 32, 128), F32), vmem((ny, 2, 4, 8, 8, 128), F32)],
        [vmem((nx, 8, 32, 128), F32), vmem((ny, 4, 8, 8, 128), F32)],
        vmem((GROUPS, 3, 8, 8, 128), F32),
        vmem((GROUPS, 8, 8, 128), F32),
        vmem((7, GROUPS, 8, 128), F32),
        vmem((GROUPS, 8, 128), F32),
        vmem((GROUPS, 4, 8, 256), F32),
        vmem((GROUPS, 4, 32, 256), F32),
        vmem((7, 4, 32, 128), F32), vmem((4, 32, 128), F32),
        vmem((3, 32, 128), F32), vmem((32, 128), F32),
        vmem((3, 8, 128), F32),
        pltpu.SemaphoreType.DMA((3,)),
        pltpu.SemaphoreType.DMA((2,)),
        pltpu.SemaphoreType.DMA((N_SEM,)),
        pltpu.SemaphoreType.DMA((N_SEM,)),
    ]
    here = pl.BlockSpec(memory_space=pl.ANY)
    held = pl.BlockSpec(memory_space=pltpu.VMEM)
    output, volume_grad, kg = pl.pallas_call(
        functools.partial(kernel, factor),
        out_shape=(vmem((256, 256), F32), vmem((256, 256), F32), vmem((27, 32, 256), F32)),
        in_specs=[here] * 3,
        out_specs=(held,) * 3,
        scratch_shapes=scratch,
        compiler_params=pltpu.CompilerParams(
            collective_id=0, has_side_effects=True, vmem_limit_bytes=56 * 2**20
        ),
    )(volume, upstream, jnp.transpose(kernel_taps, (1, 0, 2)))
    results = [
        pltpu.with_memory_space_constraint(r, pltpu.VMEM) for r in (output, volume_grad, kg)
    ]
    output, volume_grad, kg = pl.pallas_call(
        store,
        out_shape=tuple(jax.ShapeDtypeStruct(r.shape, F32) for r in results),
        in_specs=[held] * 3,
        out_specs=(here,) * 3,
        scratch_shapes=[pltpu.SemaphoreType.DMA((3,))],
    )(*results)
    return (
        output.reshape(volume.shape),
        volume_grad.reshape(volume.shape),
        jnp.transpose(kg, (1, 0, 2)),
    )


def solution(mesh):
    cells = 256 * mesh.shape["dev"] * mesh.shape["ha"] * mesh.shape["wa"]
    place = P("dev", "ha", "wa", None)
    return jax.shard_map(
        functools.partial(per_device, 1.0 / math.sqrt(cells)),
        mesh=mesh,
        in_specs=(place, P(), place),
        out_specs=(place, place, P("wa", None, None)),
        check_vma=False,
    )
```

```python
import functools
import math

import jax
import jax.numpy as jnp
from jax import lax
from jax.experimental import pallas as pl
from jax.experimental.pallas import tpu as pltpu
from jax.sharding import PartitionSpec as P

MESH = pl.DeviceIdType.MESH
F32 = jnp.float32
BF16 = jnp.bfloat16

GROUPS = 7
FIRST = ("x", "y", "z", "x", "y", "x", "y")
DEPTH = FIRST.index("z")
SLOT = (0, 1, 4, 2, 3, 5, 6)
BATCHES = ((0, 2), (2, 5), (5, 7))
N_SEM = 2 * 26 + GROUPS + 6 * (4 + 2 + 3) + (7 + 3 + 3) + len(BATCHES) * (7 + 7 + 3)


def far_first(n):
    return sorted(range(1, n), key=lambda k: -min(k, n - k))


def tap(u):
    return u + 9 if u < 9 else u - 9 if u < 18 else u


def split(x):
    hi = x.astype(BF16)
    return hi, (x - hi.astype(F32)).astype(BF16)


def dot3(lhs, rhs, dims):
    (lh, ll), (rh, rl) = lhs, rhs
    dot = functools.partial(
        lax.dot_general, dimension_numbers=(dims, ((), ())), preferred_element_type=F32
    )
    return dot(lh, rh) + (dot(ll, rh) + dot(lh, rl))


def kernel(
    factor,
    vol_ref, up_ref, k_hbm, out_ref, vg_ref, kg_ref,
    k_f, pad_v, pad_u, col_v, col_u, halo_v, halo_u,
    wv_hi, wv_lo, wu_hi, wu_lo, vt_hi, vt_lo,
    part, pair, summed, r1, s2, r2, mid, q1, low, rz, fin, agz, gathered,
    z1, zmid, z2, zlow, z3,
    ksem, local_sem, send_sem, recv_sem,
):
    z, y, w = lax.axis_index("dev"), lax.axis_index("ha"), lax.axis_index("wa")
    core = lax.rem(w, 2)
    x = lax.div(w, 2)

    def step(i, by, n):
        return lax.rem(i + (by + n), n)

    counter = [0]
    sent = []

    def copy(src, dst, device):
        i = counter[0]
        counter[0] += 1
        return pltpu.make_async_remote_copy(
            src_ref=src, dst_ref=dst, send_sem=send_sem.at[i], recv_sem=recv_sem.at[i],
            device_id=device, device_id_type=MESH,
        )

    def start(*copies):
        for c in copies:
            c.start()
            sent.append(c)
        return copies

    load_u = pltpu.make_async_copy(up_ref, pad_u.at[pl.ds(1, 4), pl.ds(1, 8)], local_sem.at[0])
    load_v = pltpu.make_async_copy(vol_ref, pad_v.at[pl.ds(1, 4), pl.ds(1, 8)], local_sem.at[1])
    load_u.start()
    load_v.start()
    around = [
        (sd, sh, sw) for sd in (0, -1, 1) for sh in (-1, 0, 1) for sw in (-1, 0, 1)
        if (sd, sh, sw) != (0, 0, 0)
    ]

    def neighbour(sd, sh, sw):
        return {"dev": step(z, sd, 8), "ha": step(y, sh, 4), "wa": step(w, sw, 8)}

    peers = [neighbour(*by) for by in around]
    for k in range(2, 7):
        peers.append({"dev": step(z, k, 8)})
    for k in (-2, 2, 4):
        peers.append({"wa": step(w, k, 8)})
    peers.append({"ha": step(y, 2, 4)})
    barrier = pltpu.get_barrier_semaphore()
    for peer in peers:
        pl.semaphore_signal(barrier, inc=1, device_id=peer, device_id_type=MESH)
    def cut_columns(pad, col):
        col[0] = pad[1:5, 1:9, 7:8, :]
        col[1] = pad[1:5, 1:9, 0:1, :]

    k_copies = [
        pltpu.make_async_copy(k_hbm.at[pl.ds(9 * i, 9)], k_f.at[pl.ds(9 * i, 9)], ksem.at[i])
        for i in range(3)
    ]
    pl.semaphore_wait(barrier, len(peers))

    def send_halo(src, pad, col, halo, pieces):
        copies = []
        for sd, sh, sw in pieces:
            d_src, d_dst, d_n = ((0, 5, 1), (0, 1, 4), (3, 0, 1))[sd + 1]
            h_src, h_dst, h_n = ((0, 9, 1), (0, 1, 8), (7, 0, 1))[sh + 1]
            at = (pl.ds(d_src, d_n), pl.ds(h_src, h_n))
            to = (pl.ds(d_dst, d_n), pl.ds(h_dst, h_n))
            if sw == 0:
                a, b = src.at[at], pad.at[to]
            else:
                side = 0 if sw == 1 else 1
                a, b = col.at[(side,) + at], halo.at[(side,) + to]
            copies.append(copy(a, b, neighbour(sd, sh, sw)))
        return start(*copies)

    def arrive(copies):
        for c in copies:
            c.wait_recv()

    def windows(pad, halo, hi_ref, lo_ref, planes):
        def body(i, carry):
            d = planes.start + i * planes.step
            rows = pl.ds(pl.multiple_of(d * 64, 64), 64)
            plane = pad[d]
            at = lax.broadcasted_iota(jnp.int32, plane.shape, 1)
            before = jnp.broadcast_to(halo[0, d], plane.shape)
            after = jnp.broadcast_to(halo[1, d], plane.shape)
            shifted = (
                jnp.where(at == 0, before, pltpu.roll(plane, 1, 1)),
                plane,
                jnp.where(at == 7, after, pltpu.roll(plane, 7, 1)),
            )
            for b in range(3):
                for c in range(3):
                    hi, lo = split(shifted[c][b : b + 8].reshape(64, plane.shape[-1]))
                    hi_ref[3 * b + c, rows, :] = hi
                    lo_ref[3 * b + c, rows, :] = lo
            return carry

        lax.fori_loop(0, len(planes), body, 0)

    def window(hi_ref, lo_ref, t):
        t = jnp.int32(t)
        rows = pl.ds(pl.multiple_of(lax.div(t, 9) * 64, 64), 256)
        i = lax.rem(t, 9)
        return hi_ref[i, rows, :], lo_ref[i, rows, :]

    def kernel_grad(g):
        taps = min(4, 27 - 4 * g)
        for i in range(taps):
            d, at = divmod(26 - tap(4 * g + i), 9)
            rows = slice(64 * d, 64 * d + 256)
            upwin = wu_hi[at, rows, :], wu_lo[at, rows, :]
            res = dot3((vt_hi[...], vt_lo[...]), upwin, ((1,), (0,)))
            for block in range(8):
                for half in range(2):
                    part[g, block % 2, block // 2, 2 * i + half] = res[
                        32 * block : 32 * block + 32, 128 * half : 128 * half + 128
                    ]
        for i in range(taps, 4):
            for j in (2 * i, 2 * i + 1):
                part[g, :, :, j] = jnp.zeros((2, 4, 32, 128), F32)
        groups[g].pair()

    def products(first, last):
        def add(taps):
            out, grad = 0.0, 0.0
            for t in taps:
                k = split(k_f[t])
                out += dot3(window(wv_hi, wv_lo, t), k, ((1,), (0,)))
                grad += dot3(window(wu_hi, wu_lo, 26 - t), k, ((1,), (1,)))
            out_ref[...] += out
            vg_ref[...] += grad

        def body(i, carry):
            add((first + 2 * i, first + 2 * i + 1))
            return carry

        lax.fori_loop(0, (last - first) // 2, body, 0)
        if (last - first) % 2:
            add((last - 1,))

    def place(axis):
        return {"x": x, "y": y, "z": z}[axis]

    def away(axis, by):
        if axis == "x":
            return {"wa": step(w, 2 * by, 8)}
        return {"ha": step(y, by, 4)} if axis == "y" else {"dev": step(z, by, 8)}

    def direct(axis, chunk, recv):
        n = 8 if axis == "z" else 4
        return start(*(
            copy(chunk(step(place(axis), k, n)), recv.at[k - 1], away(axis, k)) for k in far_first(n)
        ))

    def direct_sum(axis, copies, chunk, recv):
        arrive(copies)
        total = chunk(place(axis))[...]
        for k in range(len(copies)):
            total = total + recv[k]
        return total

    def halves(ref, h):
        if len(ref.shape) == 4:
            return ref.at[:, pl.ds(4 * h, 4)]
        return ref.at[pl.ds(4 * h, 4)]

    def ring_1(axis, chunk, recv, recv_2):
        i = place(axis)
        far, above, below = (chunk(step(i, k, 4)) for k in (2, 1, -1))
        return start(
            copy(halves(far, 0), recv.at[0], away(axis, 1)),
            copy(halves(far, 1), recv.at[1], away(axis, -1)),
        ), start(
            copy(halves(above, 1), halves(recv_2.at[0], 1), away(axis, 1)),
            copy(halves(below, 0), halves(recv_2.at[1], 0), away(axis, -1)),
        )

    def ring_2(axis, copies, chunk, recv, stage, recv_2):
        arrive(copies)
        for h, by in ((0, 1), (1, -1)):
            stage[h] = halves(chunk(step(place(axis), by, 4)), h)[...] + recv[h]
        return start(
            copy(stage.at[0], halves(recv_2.at[0], 0), away(axis, 1)),
            copy(stage.at[1], halves(recv_2.at[1], 1), away(axis, -1)),
        )

    def rows_of(ref, k):
        rows = pl.ds(pl.multiple_of(k * 8, 8), 8)
        return ref.at[(slice(None),) * (len(ref.shape) - 2) + (rows,)]

    class Group:
        def __init__(self, g):
            self.g = g
            self.slot = SLOT[g]
            self.sum = summed.at[g]

        def pair(self):
            self.c = start(copy(part.at[self.g, 1 - core], pair.at[self.g], {"wa": w + 1 - 2 * core}))

        def add_pair(self):
            arrive(self.c)
            self.sum[...] = part[self.g, core] + pair[self.g]

    class PlaneGroup(Group):
        def __init__(self, g):
            super().__init__(g)
            self.first = FIRST[g]
            self.second = "y" if self.first == "x" else "x"
            n = FIRST[:g].count(self.first)
            i = 0 if self.first == "x" else 1
            self.r1, self.s2, self.r2 = r1[i].at[n], s2[i].at[n], r2[i].at[n]
            self.mid = mid[i].at[n]
            self.q1 = q1.at[self.slot]
            if self.first == "x":
                self.chunk_1 = lambda k: self.sum.at[k]
                self.chunk_2 = lambda k: rows_of(self.mid, k)
            else:
                self.chunk_1 = lambda k: rows_of(self.sum, k)
                self.chunk_2 = lambda k: self.mid.at[k]

        def e1(self):
            self.add_pair()
            self.c, self.near = ring_1(self.first, self.chunk_1, self.r1, self.r2)

        def e2(self):
            self.c = ring_2(self.first, self.c, self.chunk_1, self.r1, self.s2, self.r2)

        def e3(self):
            arrive(self.near)
            self.mid[...] = direct_sum(self.first, self.c, self.chunk_1, self.r2)
            self.c = direct(self.second, self.chunk_2, self.q1)

        def e4(self):
            low[self.slot] = direct_sum(self.second, self.c, self.chunk_2, self.q1)

    class DepthGroup(Group):
        def __init__(self, g):
            super().__init__(g)
            self.chunk_1 = lambda k: self.sum.at[:, k]
            self.chunk_2 = lambda k: zmid.at[k]
            self.chunk_3 = lambda k: rows_of(zlow, k)

        def e1(self):
            self.add_pair()
            self.c = direct("z", self.chunk_1, z1)

        def e2(self):
            zmid[...] = direct_sum("z", self.c, self.chunk_1, z1)
            self.c = direct("x", self.chunk_2, z2)

        def e3(self):
            zlow[...] = direct_sum("x", self.c, self.chunk_2, z2)
            self.c = direct("y", self.chunk_3, z3)

        def result(self):
            return direct_sum("y", self.c, self.chunk_3, z3)

    class Batch:
        def __init__(self, i):
            self.i = i
            lo, hi = BATCHES[i]
            self.depth_group = hi == SLOT[DEPTH] + 1
            self.n = hi - lo - (1 if self.depth_group else 0)
            self.lo = lo
            self.sums = pl.ds(lo, self.n)
            self.all = pl.ds(lo, hi - lo)

        def e6(self):
            self.c = start(*(
                copy(low.at[self.sums, step(z, k, 8)], rz.at[k - 1, self.sums], {"dev": step(z, k, 8)})
                for k in far_first(8)
            ))

        def e7(self):
            arrive(self.c)
            total = low[self.sums, z]
            for k in range(7):
                total = total + rz[k, self.sums]
            fin[self.sums] = total * factor
            if self.depth_group:
                fin[SLOT[DEPTH]] = groups[DEPTH].result() * factor
            agz_at = lambda k: agz.at[
                self.all, lax.div(k, 2), :, pl.ds(pl.multiple_of(lax.rem(k, 2) * 128, 128), 128)
            ]
            agz_at(z)[...] = fin[self.all]
            first = counter[0]
            start(*(copy(fin.at[self.all], agz_at(z), {"dev": step(z, k, 8)}) for k in far_first(8)))
            self.c = [
                self.landed(first + i, agz_at(step(z, -k, 8)), {"dev": step(z, k, 8)})
                for i, k in enumerate(far_first(8))
            ]

        def landed(self, i, slot, device):
            return pltpu.make_async_remote_copy(
                src_ref=slot, dst_ref=slot, send_sem=send_sem.at[i], recv_sem=recv_sem.at[i],
                device_id=device, device_id_type=MESH,
            )

        def e8(self):
            arrive(self.c)
            first = counter[0]
            here = agz.at[self.all]
            there = lambda k: rows_of(gathered.at[self.all], k)
            there(y)[...] = agz[self.all]
            start(*(copy(here, there(y), {"ha": step(y, k, 4)}) for k in far_first(4)))
            self.c = [
                self.landed(first + i, there(step(y, -k, 4)), {"ha": step(y, k, 4)})
                for i, k in enumerate(far_first(4))
            ]

        def e9(self):
            arrive(self.c)
            for u in range(27):
                if BATCHES[self.i][0] <= SLOT[u // 4] < BATCHES[self.i][1]:
                    kg_ref[tap(u)] = gathered[SLOT[u // 4], u % 4]

    groups = [(DepthGroup if FIRST[g] == "z" else PlaneGroup)(g) for g in range(GROUPS)]
    batches = [Batch(i) for i in range(len(BATCHES))]

    inner = [by for by in around if by[2] == 0]
    outer = [by for by in around if by[2] != 0]
    flat_u = send_halo(up_ref, pad_u, col_u, halo_u, inner[:2])
    deep_u = send_halo(up_ref, pad_u, col_u, halo_u, inner[2:])
    load_u.wait()
    cut_columns(pad_u, col_u)
    flat_u += send_halo(up_ref, pad_u, col_u, halo_u, outer[:6])
    deep_u += send_halo(up_ref, pad_u, col_u, halo_u, outer[6:])
    for c in k_copies:
        c.start()
    load_v.wait()
    cut_columns(pad_v, col_v)
    hi, lo = split(pad_v[1:5, 1:9].reshape(256, 256).T)
    vt_hi[...] = hi
    vt_lo[...] = lo
    out_ref[...] = jnp.zeros_like(out_ref)
    vg_ref[...] = jnp.zeros_like(vg_ref)
    arrive(flat_u)
    halos_v = send_halo(vol_ref, pad_v, col_v, halo_v, around)
    windows(pad_u, halo_u, wu_hi, wu_lo, range(1, 5))
    kernel_grad(0)
    kernel_grad(1)
    arrive(deep_u)
    windows(pad_u, halo_u, wu_hi, wu_lo, range(0, 6, 5))
    kernel_grad(2)
    groups[0].e1()
    kernel_grad(3)
    groups[1].e1()
    kernel_grad(4)
    groups[2].e1()
    groups[3].e1()
    kernel_grad(5)
    groups[4].e1()
    kernel_grad(6)
    groups[5].e1()
    groups[6].e1()
    groups[0].e2()
    groups[1].e2()
    groups[3].e2()
    groups[4].e2()
    arrive(halos_v)
    windows(pad_v, halo_v, wv_hi, wv_lo, range(6))
    groups[5].e2()
    groups[6].e2()
    for c in k_copies:
        c.wait()
    products(0, 4)
    groups[0].e3()
    groups[1].e3()
    products(4, 8)
    groups[3].e3()
    groups[4].e3()
    products(8, 10)
    groups[0].e4()
    groups[1].e4()
    batches[0].e6()
    products(10, 12)
    groups[5].e3()
    groups[6].e3()
    groups[2].e2()
    products(12, 14)
    groups[3].e4()
    groups[4].e4()
    batches[1].e6()
    products(14, 18)
    groups[2].e3()
    groups[5].e4()
    groups[6].e4()
    batches[2].e6()
    batches[0].e7()
    products(18, 22)
    batches[1].e7()
    batches[2].e7()
    batches[0].e8()
    products(22, 27)
    batches[1].e8()
    batches[2].e8()
    for batch in batches:
        batch.e9()
    assert counter[0] == N_SEM, counter[0]
    for c in sent:
        c.wait_send()


def store(out_in, vg_in, kg_in, out_ref, vg_ref, kg_ref, sem):
    copies = [
        pltpu.make_async_copy(src, dst, sem.at[i])
        for i, (src, dst) in enumerate(((kg_in, kg_ref), (out_in, out_ref), (vg_in, vg_ref)))
    ]
    for c in copies:
        c.start()
    for c in copies:
        c.wait()


def per_device(factor, volume, kernel_taps, upstream):
    nx, ny = FIRST.count("x"), FIRST.count("y")
    vmem = pltpu.VMEM
    scratch = [
        vmem((27, 256, 256), F32),
        vmem((6, 10, 8, 256), F32), vmem((6, 10, 8, 256), F32),
        vmem((2, 4, 8, 1, 256), F32), vmem((2, 4, 8, 1, 256), F32),
        vmem((2, 6, 10, 1, 256), F32), vmem((2, 6, 10, 1, 256), F32),
        vmem((9, 384, 256), BF16), vmem((9, 384, 256), BF16),
        vmem((9, 384, 256), BF16), vmem((9, 384, 256), BF16),
        vmem((256, 256), BF16), vmem((256, 256), BF16),
        vmem((GROUPS, 2, 4, 8, 32, 128), F32),
        vmem((GROUPS, 4, 8, 32, 128), F32),
        vmem((GROUPS, 4, 8, 32, 128), F32),
        [vmem((nx, 2, 4, 32, 128), F32), vmem((ny, 2, 4, 4, 8, 128), F32)],
        [vmem((nx, 2, 4, 32, 128), F32), vmem((ny, 2, 4, 4, 8, 128), F32)],
        [vmem((nx, 2, 8, 32, 128), F32), vmem((ny, 2, 4, 8, 8, 128), F32)],
        [vmem((nx, 8, 32, 128), F32), vmem((ny, 4, 8, 8, 128), F32)],
        vmem((GROUPS, 3, 8, 8, 128), F32),
        vmem((GROUPS, 8, 8, 128), F32),
        vmem((7, GROUPS, 8, 128), F32),
        vmem((GROUPS, 8, 128), F32),
        vmem((GROUPS, 4, 8, 256), F32),
        vmem((GROUPS, 4, 32, 256), F32),
        vmem((7, 4, 32, 128), F32), vmem((4, 32, 128), F32),
        vmem((3, 32, 128), F32), vmem((32, 128), F32),
        vmem((3, 8, 128), F32),
        pltpu.SemaphoreType.DMA((3,)),
        pltpu.SemaphoreType.DMA((2,)),
        pltpu.SemaphoreType.DMA((N_SEM,)),
        pltpu.SemaphoreType.DMA((N_SEM,)),
    ]
    here = pl.BlockSpec(memory_space=pl.ANY)
    held = pl.BlockSpec(memory_space=pltpu.VMEM)
    output, volume_grad, kg = pl.pallas_call(
        functools.partial(kernel, factor),
        out_shape=(vmem((256, 256), F32), vmem((256, 256), F32), vmem((27, 32, 256), F32)),
        in_specs=[here] * 3,
        out_specs=(held,) * 3,
        scratch_shapes=scratch,
        compiler_params=pltpu.CompilerParams(
            collective_id=0, has_side_effects=True, vmem_limit_bytes=56 * 2**20
        ),
    )(volume, upstream, jnp.transpose(kernel_taps, (1, 0, 2)))
    results = [
        pltpu.with_memory_space_constraint(r, pltpu.VMEM) for r in (output, volume_grad, kg)
    ]
    output, volume_grad, kg = pl.pallas_call(
        store,
        out_shape=tuple(jax.ShapeDtypeStruct(r.shape, F32) for r in results),
        in_specs=[held] * 3,
        out_specs=(here,) * 3,
        scratch_shapes=[pltpu.SemaphoreType.DMA((3,))],
    )(*results)
    return (
        output.reshape(volume.shape),
        volume_grad.reshape(volume.shape),
        jnp.transpose(kg, (1, 0, 2)),
    )


def solution(mesh):
    cells = 256 * mesh.shape["dev"] * mesh.shape["ha"] * mesh.shape["wa"]
    place = P("dev", "ha", "wa", None)
    return jax.shard_map(
        functools.partial(per_device, 1.0 / math.sqrt(cells)),
        mesh=mesh,
        in_specs=(place, P(), place),
        out_specs=(place, place, P("wa", None, None)),
        check_vma=False,
    )
```

```python
import functools
import math

import jax
import jax.numpy as jnp
from jax import lax
from jax.experimental import pallas as pl
from jax.experimental.pallas import tpu as pltpu
from jax.sharding import PartitionSpec as P

MESH = pl.DeviceIdType.MESH
F32 = jnp.float32
BF16 = jnp.bfloat16

GROUPS = 7
FIRST = ("x", "y", "z", "x", "y", "x", "y")
DEPTH = FIRST.index("z")
SLOT = (0, 1, 4, 2, 3, 5, 6)
BATCHES = ((0, 2), (2, 5), (5, 7))
N_SEM = 2 * 26 + 2 * GROUPS + 6 * (4 + 2 + 3) + (7 + 3 + 3) + len(BATCHES) * (7 + 7 + 3)


def far_first(n):
    return sorted(range(1, n), key=lambda k: -min(k, n - k))


def tap(u):
    return u + 9 if u < 9 else u - 9 if u < 18 else u


def split(x):
    hi = x.astype(BF16)
    return hi, (x - hi.astype(F32)).astype(BF16)


def dot3(lhs, rhs, dims):
    (lh, ll), (rh, rl) = lhs, rhs
    dot = functools.partial(
        lax.dot_general, dimension_numbers=(dims, ((), ())), preferred_element_type=F32
    )
    return dot(lh, rh) + (dot(ll, rh) + dot(lh, rl))


def kernel(
    factor,
    vol_ref, up_ref, k_hbm, out_ref, vg_ref, kg_ref,
    k_f, pad_v, pad_u, col_v, col_u, halo_v, halo_u,
    wv_hi, wv_lo, wu_hi, wu_lo, vt_hi, vt_lo,
    part, pair, summed, r1, s2, r2, mid, q1, low, rz, fin, agz, gathered,
    z1, zmid, z2, zlow, z3,
    ksem, local_sem, send_sem, recv_sem,
):
    z, y, w = lax.axis_index("dev"), lax.axis_index("ha"), lax.axis_index("wa")
    core = lax.rem(w, 2)
    x = lax.div(w, 2)

    def step(i, by, n):
        return lax.rem(i + (by + n), n)

    counter = [0]
    sent = []

    def copy(src, dst, device):
        i = counter[0]
        counter[0] += 1
        return pltpu.make_async_remote_copy(
            src_ref=src, dst_ref=dst, send_sem=send_sem.at[i], recv_sem=recv_sem.at[i],
            device_id=device, device_id_type=MESH,
        )

    def start(*copies):
        for c in copies:
            c.start()
            sent.append(c)
        return copies

    load_u = pltpu.make_async_copy(up_ref, pad_u.at[pl.ds(1, 4), pl.ds(1, 8)], local_sem.at[0])
    load_v = pltpu.make_async_copy(vol_ref, pad_v.at[pl.ds(1, 4), pl.ds(1, 8)], local_sem.at[1])
    load_u.start()
    load_v.start()
    around = [
        (sd, sh, sw) for sd in (0, -1, 1) for sh in (-1, 0, 1) for sw in (-1, 0, 1)
        if (sd, sh, sw) != (0, 0, 0)
    ]

    def neighbour(sd, sh, sw):
        return {"dev": step(z, sd, 8), "ha": step(y, sh, 4), "wa": step(w, sw, 8)}

    peers = [neighbour(*by) for by in around]
    for k in range(2, 7):
        peers.append({"dev": step(z, k, 8)})
    for k in (-2, 2, 4):
        peers.append({"wa": step(w, k, 8)})
    peers.append({"ha": step(y, 2, 4)})
    barrier = pltpu.get_barrier_semaphore()
    for peer in peers:
        pl.semaphore_signal(barrier, inc=1, device_id=peer, device_id_type=MESH)
    def cut_columns(pad, col):
        col[0] = pad[1:5, 1:9, 7:8, :]
        col[1] = pad[1:5, 1:9, 0:1, :]

    k_copies = [
        pltpu.make_async_copy(k_hbm.at[pl.ds(9 * i, 9)], k_f.at[pl.ds(9 * i, 9)], ksem.at[i])
        for i in range(3)
    ]
    pl.semaphore_wait(barrier, len(peers))

    def send_halo(src, pad, col, halo, pieces):
        copies = []
        for sd, sh, sw in pieces:
            d_src, d_dst, d_n = ((0, 5, 1), (0, 1, 4), (3, 0, 1))[sd + 1]
            h_src, h_dst, h_n = ((0, 9, 1), (0, 1, 8), (7, 0, 1))[sh + 1]
            at = (pl.ds(d_src, d_n), pl.ds(h_src, h_n))
            to = (pl.ds(d_dst, d_n), pl.ds(h_dst, h_n))
            if sw == 0:
                a, b = src.at[at], pad.at[to]
            else:
                side = 0 if sw == 1 else 1
                a, b = col.at[(side,) + at], halo.at[(side,) + to]
            copies.append(copy(a, b, neighbour(sd, sh, sw)))
        return start(*copies)

    def arrive(copies):
        for c in copies:
            c.wait_recv()

    def windows(pad, halo, hi_ref, lo_ref, planes):
        def body(i, carry):
            d = planes.start + i * planes.step
            rows = pl.ds(pl.multiple_of(d * 64, 64), 64)
            plane = pad[d]
            at = lax.broadcasted_iota(jnp.int32, plane.shape, 1)
            before = jnp.broadcast_to(halo[0, d], plane.shape)
            after = jnp.broadcast_to(halo[1, d], plane.shape)
            shifted = (
                jnp.where(at == 0, before, pltpu.roll(plane, 1, 1)),
                plane,
                jnp.where(at == 7, after, pltpu.roll(plane, 7, 1)),
            )
            for b in range(3):
                for c in range(3):
                    hi, lo = split(shifted[c][b : b + 8].reshape(64, plane.shape[-1]))
                    hi_ref[3 * b + c, rows, :] = hi
                    lo_ref[3 * b + c, rows, :] = lo
            return carry

        lax.fori_loop(0, len(planes), body, 0)

    def window(hi_ref, lo_ref, t):
        t = jnp.int32(t)
        rows = pl.ds(pl.multiple_of(lax.div(t, 9) * 64, 64), 256)
        i = lax.rem(t, 9)
        return hi_ref[i, rows, :], lo_ref[i, rows, :]

    def kernel_grad(g):
        taps = min(4, 27 - 4 * g)
        for i in range(taps):
            d, at = divmod(26 - tap(4 * g + i), 9)
            rows = slice(64 * d, 64 * d + 256)
            upwin = wu_hi[at, rows, :], wu_lo[at, rows, :]
            res = dot3((vt_hi[...], vt_lo[...]), upwin, ((1,), (0,)))
            for block in range(8):
                for half in range(2):
                    part[g, block % 2, block // 2, 2 * i + half] = res[
                        32 * block : 32 * block + 32, 128 * half : 128 * half + 128
                    ]
            if i == 1:
                groups[g].pair()
        for i in range(taps, 4):
            for j in (2 * i, 2 * i + 1):
                part[g, :, :, j] = jnp.zeros((2, 4, 32, 128), F32)
        groups[g].pair()

    def products(first, last):
        def add(taps):
            out, grad = 0.0, 0.0
            for t in taps:
                k = split(k_f[t])
                out += dot3(window(wv_hi, wv_lo, t), k, ((1,), (0,)))
                grad += dot3(window(wu_hi, wu_lo, 26 - t), k, ((1,), (1,)))
            out_ref[...] += out
            vg_ref[...] += grad

        def body(i, carry):
            add((first + 2 * i, first + 2 * i + 1))
            return carry

        lax.fori_loop(0, (last - first) // 2, body, 0)
        if (last - first) % 2:
            add((last - 1,))

    def place(axis):
        return {"x": x, "y": y, "z": z}[axis]

    def away(axis, by):
        if axis == "x":
            return {"wa": step(w, 2 * by, 8)}
        return {"ha": step(y, by, 4)} if axis == "y" else {"dev": step(z, by, 8)}

    def direct(axis, chunk, recv):
        n = 8 if axis == "z" else 4
        return start(*(
            copy(chunk(step(place(axis), k, n)), recv.at[k - 1], away(axis, k)) for k in far_first(n)
        ))

    def direct_sum(axis, copies, chunk, recv):
        arrive(copies)
        total = chunk(place(axis))[...]
        for k in range(len(copies)):
            total = total + recv[k]
        return total

    def halves(ref, h):
        if len(ref.shape) == 4:
            return ref.at[:, pl.ds(4 * h, 4)]
        return ref.at[pl.ds(4 * h, 4)]

    def ring_1(axis, chunk, recv, recv_2):
        i = place(axis)
        far, above, below = (chunk(step(i, k, 4)) for k in (2, 1, -1))
        return start(
            copy(halves(far, 0), recv.at[0], away(axis, 1)),
            copy(halves(far, 1), recv.at[1], away(axis, -1)),
        ), start(
            copy(halves(above, 1), halves(recv_2.at[0], 1), away(axis, 1)),
            copy(halves(below, 0), halves(recv_2.at[1], 0), away(axis, -1)),
        )

    def ring_2(axis, copies, chunk, recv, stage, recv_2):
        arrive(copies)
        for h, by in ((0, 1), (1, -1)):
            stage[h] = halves(chunk(step(place(axis), by, 4)), h)[...] + recv[h]
        return start(
            copy(stage.at[0], halves(recv_2.at[0], 0), away(axis, 1)),
            copy(stage.at[1], halves(recv_2.at[1], 1), away(axis, -1)),
        )

    def rows_of(ref, k):
        rows = pl.ds(pl.multiple_of(k * 8, 8), 8)
        return ref.at[(slice(None),) * (len(ref.shape) - 2) + (rows,)]

    class Group:
        def __init__(self, g):
            self.g = g
            self.slot = SLOT[g]
            self.sum = summed.at[g]
            self.pairs = ()

        def pair(self):
            h = len(self.pairs)
            self.pairs += start(copy(
                part.at[self.g, 1 - core, :, pl.ds(4 * h, 4)], pair.at[self.g, :, pl.ds(4 * h, 4)],
                {"wa": w + 1 - 2 * core},
            ))

        def add_pair(self):
            arrive(self.pairs)
            self.sum[...] = part[self.g, core] + pair[self.g]

    class PlaneGroup(Group):
        def __init__(self, g):
            super().__init__(g)
            self.first = FIRST[g]
            self.second = "y" if self.first == "x" else "x"
            n = FIRST[:g].count(self.first)
            i = 0 if self.first == "x" else 1
            self.r1, self.s2, self.r2 = r1[i].at[n], s2[i].at[n], r2[i].at[n]
            self.mid = mid[i].at[n]
            self.q1 = q1.at[self.slot]
            if self.first == "x":
                self.chunk_1 = lambda k: self.sum.at[k]
                self.chunk_2 = lambda k: rows_of(self.mid, k)
            else:
                self.chunk_1 = lambda k: rows_of(self.sum, k)
                self.chunk_2 = lambda k: self.mid.at[k]

        def e1(self):
            self.add_pair()
            self.c, self.near = ring_1(self.first, self.chunk_1, self.r1, self.r2)

        def e2(self):
            self.c = ring_2(self.first, self.c, self.chunk_1, self.r1, self.s2, self.r2)

        def e3(self):
            arrive(self.near)
            self.mid[...] = direct_sum(self.first, self.c, self.chunk_1, self.r2)
            self.c = direct(self.second, self.chunk_2, self.q1)

        def e4(self):
            low[self.slot] = direct_sum(self.second, self.c, self.chunk_2, self.q1)

    class DepthGroup(Group):
        def __init__(self, g):
            super().__init__(g)
            self.chunk_1 = lambda k: self.sum.at[:, k]
            self.chunk_2 = lambda k: zmid.at[k]
            self.chunk_3 = lambda k: rows_of(zlow, k)

        def e1(self):
            self.add_pair()
            self.c = direct("z", self.chunk_1, z1)

        def e2(self):
            zmid[...] = direct_sum("z", self.c, self.chunk_1, z1)
            self.c = direct("x", self.chunk_2, z2)

        def e3(self):
            zlow[...] = direct_sum("x", self.c, self.chunk_2, z2)
            self.c = direct("y", self.chunk_3, z3)

        def result(self):
            return direct_sum("y", self.c, self.chunk_3, z3)

    class Batch:
        def __init__(self, i):
            self.i = i
            lo, hi = BATCHES[i]
            self.depth_group = hi == SLOT[DEPTH] + 1
            self.n = hi - lo - (1 if self.depth_group else 0)
            self.lo = lo
            self.sums = pl.ds(lo, self.n)
            self.all = pl.ds(lo, hi - lo)

        def e6(self):
            self.c = start(*(
                copy(low.at[self.sums, step(z, k, 8)], rz.at[k - 1, self.sums], {"dev": step(z, k, 8)})
                for k in far_first(8)
            ))

        def e7(self):
            arrive(self.c)
            total = low[self.sums, z]
            for k in range(7):
                total = total + rz[k, self.sums]
            fin[self.sums] = total * factor
            if self.depth_group:
                fin[SLOT[DEPTH]] = groups[DEPTH].result() * factor
            agz_at = lambda k: agz.at[
                self.all, lax.div(k, 2), :, pl.ds(pl.multiple_of(lax.rem(k, 2) * 128, 128), 128)
            ]
            agz_at(z)[...] = fin[self.all]
            first = counter[0]
            start(*(copy(fin.at[self.all], agz_at(z), {"dev": step(z, k, 8)}) for k in far_first(8)))
            self.c = [
                self.landed(first + i, agz_at(step(z, -k, 8)), {"dev": step(z, k, 8)})
                for i, k in enumerate(far_first(8))
            ]

        def landed(self, i, slot, device):
            return pltpu.make_async_remote_copy(
                src_ref=slot, dst_ref=slot, send_sem=send_sem.at[i], recv_sem=recv_sem.at[i],
                device_id=device, device_id_type=MESH,
            )

        def e8(self):
            arrive(self.c)
            first = counter[0]
            here = agz.at[self.all]
            there = lambda k: rows_of(gathered.at[self.all], k)
            there(y)[...] = agz[self.all]
            start(*(copy(here, there(y), {"ha": step(y, k, 4)}) for k in far_first(4)))
            self.c = [
                self.landed(first + i, there(step(y, -k, 4)), {"ha": step(y, k, 4)})
                for i, k in enumerate(far_first(4))
            ]

        def e9(self):
            arrive(self.c)
            for u in range(27):
                if BATCHES[self.i][0] <= SLOT[u // 4] < BATCHES[self.i][1]:
                    kg_ref[tap(u)] = gathered[SLOT[u // 4], u % 4]

    groups = [(DepthGroup if FIRST[g] == "z" else PlaneGroup)(g) for g in range(GROUPS)]
    batches = [Batch(i) for i in range(len(BATCHES))]

    inner = [by for by in around if by[2] == 0]
    outer = [by for by in around if by[2] != 0]
    flat_u = send_halo(up_ref, pad_u, col_u, halo_u, inner[:2])
    deep_u = send_halo(up_ref, pad_u, col_u, halo_u, inner[2:])
    load_u.wait()
    cut_columns(pad_u, col_u)
    flat_u += send_halo(up_ref, pad_u, col_u, halo_u, outer[:6])
    deep_u += send_halo(up_ref, pad_u, col_u, halo_u, outer[6:])
    for c in k_copies:
        c.start()
    load_v.wait()
    cut_columns(pad_v, col_v)
    hi, lo = split(pad_v[1:5, 1:9].reshape(256, 256).T)
    vt_hi[...] = hi
    vt_lo[...] = lo
    out_ref[...] = jnp.zeros_like(out_ref)
    vg_ref[...] = jnp.zeros_like(vg_ref)
    arrive(flat_u)
    halos_v = send_halo(vol_ref, pad_v, col_v, halo_v, around)
    windows(pad_u, halo_u, wu_hi, wu_lo, range(1, 5))
    kernel_grad(0)
    kernel_grad(1)
    arrive(deep_u)
    windows(pad_u, halo_u, wu_hi, wu_lo, range(0, 6, 5))
    groups[0].e1()
    kernel_grad(2)
    groups[1].e1()
    kernel_grad(3)
    groups[2].e1()
    kernel_grad(4)
    groups[3].e1()
    kernel_grad(5)
    groups[4].e1()
    kernel_grad(6)
    groups[5].e1()
    groups[6].e1()
    groups[0].e2()
    groups[1].e2()
    groups[3].e2()
    groups[4].e2()
    arrive(halos_v)
    windows(pad_v, halo_v, wv_hi, wv_lo, range(6))
    groups[5].e2()
    groups[6].e2()
    for c in k_copies:
        c.wait()
    products(0, 4)
    groups[0].e3()
    groups[1].e3()
    products(4, 8)
    groups[3].e3()
    groups[4].e3()
    products(8, 10)
    groups[0].e4()
    groups[1].e4()
    batches[0].e6()
    products(10, 12)
    groups[5].e3()
    groups[6].e3()
    groups[2].e2()
    products(12, 14)
    groups[3].e4()
    groups[4].e4()
    batches[1].e6()
    products(14, 18)
    groups[2].e3()
    groups[5].e4()
    groups[6].e4()
    batches[2].e6()
    batches[0].e7()
    products(18, 22)
    batches[1].e7()
    batches[2].e7()
    batches[0].e8()
    products(22, 27)
    batches[1].e8()
    batches[2].e8()
    for batch in batches:
        batch.e9()
    assert counter[0] == N_SEM, counter[0]
    for c in sent:
        c.wait_send()


def store(out_in, vg_in, kg_in, out_ref, vg_ref, kg_ref, sem):
    copies = [
        pltpu.make_async_copy(src, dst, sem.at[i])
        for i, (src, dst) in enumerate(((kg_in, kg_ref), (out_in, out_ref), (vg_in, vg_ref)))
    ]
    for c in copies:
        c.start()
    for c in copies:
        c.wait()


def per_device(factor, volume, kernel_taps, upstream):
    nx, ny = FIRST.count("x"), FIRST.count("y")
    vmem = pltpu.VMEM
    scratch = [
        vmem((27, 256, 256), F32),
        vmem((6, 10, 8, 256), F32), vmem((6, 10, 8, 256), F32),
        vmem((2, 4, 8, 1, 256), F32), vmem((2, 4, 8, 1, 256), F32),
        vmem((2, 6, 10, 1, 256), F32), vmem((2, 6, 10, 1, 256), F32),
        vmem((9, 384, 256), BF16), vmem((9, 384, 256), BF16),
        vmem((9, 384, 256), BF16), vmem((9, 384, 256), BF16),
        vmem((256, 256), BF16), vmem((256, 256), BF16),
        vmem((GROUPS, 2, 4, 8, 32, 128), F32),
        vmem((GROUPS, 4, 8, 32, 128), F32),
        vmem((GROUPS, 4, 8, 32, 128), F32),
        [vmem((nx, 2, 4, 32, 128), F32), vmem((ny, 2, 4, 4, 8, 128), F32)],
        [vmem((nx, 2, 4, 32, 128), F32), vmem((ny, 2, 4, 4, 8, 128), F32)],
        [vmem((nx, 2, 8, 32, 128), F32), vmem((ny, 2, 4, 8, 8, 128), F32)],
        [vmem((nx, 8, 32, 128), F32), vmem((ny, 4, 8, 8, 128), F32)],
        vmem((GROUPS, 3, 8, 8, 128), F32),
        vmem((GROUPS, 8, 8, 128), F32),
        vmem((7, GROUPS, 8, 128), F32),
        vmem((GROUPS, 8, 128), F32),
        vmem((GROUPS, 4, 8, 256), F32),
        vmem((GROUPS, 4, 32, 256), F32),
        vmem((7, 4, 32, 128), F32), vmem((4, 32, 128), F32),
        vmem((3, 32, 128), F32), vmem((32, 128), F32),
        vmem((3, 8, 128), F32),
        pltpu.SemaphoreType.DMA((3,)),
        pltpu.SemaphoreType.DMA((2,)),
        pltpu.SemaphoreType.DMA((N_SEM,)),
        pltpu.SemaphoreType.DMA((N_SEM,)),
    ]
    here = pl.BlockSpec(memory_space=pl.ANY)
    held = pl.BlockSpec(memory_space=pltpu.VMEM)
    output, volume_grad, kg = pl.pallas_call(
        functools.partial(kernel, factor),
        out_shape=(vmem((256, 256), F32), vmem((256, 256), F32), vmem((27, 32, 256), F32)),
        in_specs=[here] * 3,
        out_specs=(held,) * 3,
        scratch_shapes=scratch,
        compiler_params=pltpu.CompilerParams(
            collective_id=0, has_side_effects=True, vmem_limit_bytes=56 * 2**20
        ),
    )(volume, upstream, jnp.transpose(kernel_taps, (1, 0, 2)))
    results = [
        pltpu.with_memory_space_constraint(r, pltpu.VMEM) for r in (output, volume_grad, kg)
    ]
    output, volume_grad, kg = pl.pallas_call(
        store,
        out_shape=tuple(jax.ShapeDtypeStruct(r.shape, F32) for r in results),
        in_specs=[held] * 3,
        out_specs=(here,) * 3,
        scratch_shapes=[pltpu.SemaphoreType.DMA((3,))],
    )(*results)
    return (
        output.reshape(volume.shape),
        volume_grad.reshape(volume.shape),
        jnp.transpose(kg, (1, 0, 2)),
    )


def solution(mesh):
    cells = 256 * mesh.shape["dev"] * mesh.shape["ha"] * mesh.shape["wa"]
    place = P("dev", "ha", "wa", None)
    return jax.shard_map(
        functools.partial(per_device, 1.0 / math.sqrt(cells)),
        mesh=mesh,
        in_specs=(place, P(), place),
        out_specs=(place, place, P("wa", None, None)),
        check_vma=False,
    )
```

```python
import functools
import math

import jax
import jax.numpy as jnp
from jax import lax
from jax.experimental import pallas as pl
from jax.experimental.pallas import tpu as pltpu
from jax.sharding import PartitionSpec as P

MESH = pl.DeviceIdType.MESH
F32 = jnp.float32
BF16 = jnp.bfloat16

GROUPS = 7
FIRST = ("x", "y", "z", "x", "y", "x", "y")
DEPTH = FIRST.index("z")
SLOT = (0, 1, 4, 2, 3, 5, 6)
BATCHES = ((0, 2), (2, 5), (5, 7))
N_SEM = 2 * 26 + GROUPS + 6 * (4 + 2 + 3) + (7 + 3 + 3) + len(BATCHES) * (7 + 7 + 3)


def far_first(n):
    return sorted(range(1, n), key=lambda k: -min(k, n - k))


def tap(u):
    return u + 9 if u < 9 else u - 9 if u < 18 else u


def split(x):
    hi = x.astype(BF16)
    return hi, (x - hi.astype(F32)).astype(BF16)


def dot3(lhs, rhs, dims):
    (lh, ll), (rh, rl) = lhs, rhs
    dot = functools.partial(
        lax.dot_general, dimension_numbers=(dims, ((), ())), preferred_element_type=F32
    )
    return dot(lh, rh) + (dot(ll, rh) + dot(lh, rl))


def kernel(
    factor,
    vol_ref, up_ref, k_hbm, out_ref, vg_ref, kg_ref,
    k_f, pad_v, pad_u, col_v, col_u, halo_v, halo_u,
    wv_hi, wv_lo, wu_hi, wu_lo, vt_hi, vt_lo,
    part, pair, summed, r1, s2, r2, mid, q1, low, rz, fin, agz, gathered,
    z1, zmid, z2, zlow, z3,
    ksem, local_sem, send_sem, recv_sem,
):
    z, y, w = lax.axis_index("dev"), lax.axis_index("ha"), lax.axis_index("wa")
    core = lax.rem(w, 2)
    x = lax.div(w, 2)

    def step(i, by, n):
        return lax.rem(i + (by + n), n)

    counter = [0]
    sent = []

    def copy(src, dst, device):
        i = counter[0]
        counter[0] += 1
        return pltpu.make_async_remote_copy(
            src_ref=src, dst_ref=dst, send_sem=send_sem.at[i], recv_sem=recv_sem.at[i],
            device_id=device, device_id_type=MESH,
        )

    def start(*copies):
        for c in copies:
            c.start()
            sent.append(c)
        return copies

    load_u = pltpu.make_async_copy(up_ref, pad_u.at[pl.ds(1, 4), pl.ds(1, 8)], local_sem.at[0])
    load_v = pltpu.make_async_copy(vol_ref, pad_v.at[pl.ds(1, 4), pl.ds(1, 8)], local_sem.at[1])
    load_u.start()
    load_v.start()
    around = [
        (sd, sh, sw) for sd in (0, -1, 1) for sh in (-1, 0, 1) for sw in (-1, 0, 1)
        if (sd, sh, sw) != (0, 0, 0)
    ]

    def neighbour(sd, sh, sw):
        return {"dev": step(z, sd, 8), "ha": step(y, sh, 4), "wa": step(w, sw, 8)}

    peers = [neighbour(*by) for by in around]
    for k in range(2, 7):
        peers.append({"dev": step(z, k, 8)})
    for k in (-2, 2, 4):
        peers.append({"wa": step(w, k, 8)})
    peers.append({"ha": step(y, 2, 4)})
    barrier = pltpu.get_barrier_semaphore()
    for peer in peers:
        pl.semaphore_signal(barrier, inc=1, device_id=peer, device_id_type=MESH)
    def cut_columns(pad, col):
        col[0] = pad[1:5, 1:9, 7:8, :]
        col[1] = pad[1:5, 1:9, 0:1, :]

    k_copies = [
        pltpu.make_async_copy(k_hbm.at[pl.ds(9 * i, 9)], k_f.at[pl.ds(9 * i, 9)], ksem.at[i])
        for i in range(3)
    ]
    pl.semaphore_wait(barrier, len(peers))

    def send_halo(src, pad, col, halo, pieces):
        copies = []
        for sd, sh, sw in pieces:
            d_src, d_dst, d_n = ((0, 5, 1), (0, 1, 4), (3, 0, 1))[sd + 1]
            h_src, h_dst, h_n = ((0, 9, 1), (0, 1, 8), (7, 0, 1))[sh + 1]
            at = (pl.ds(d_src, d_n), pl.ds(h_src, h_n))
            to = (pl.ds(d_dst, d_n), pl.ds(h_dst, h_n))
            if sw == 0:
                a, b = src.at[at], pad.at[to]
            else:
                side = 0 if sw == 1 else 1
                a, b = col.at[(side,) + at], halo.at[(side,) + to]
            copies.append(copy(a, b, neighbour(sd, sh, sw)))
        return start(*copies)

    def arrive(copies):
        for c in copies:
            c.wait_recv()

    def windows(pad, halo, hi_ref, lo_ref, planes):
        def body(i, carry):
            d = planes.start + i * planes.step
            rows = pl.ds(pl.multiple_of(d * 64, 64), 64)
            plane = pad[d]
            at = lax.broadcasted_iota(jnp.int32, plane.shape, 1)
            before = jnp.broadcast_to(halo[0, d], plane.shape)
            after = jnp.broadcast_to(halo[1, d], plane.shape)
            shifted = (
                jnp.where(at == 0, before, pltpu.roll(plane, 1, 1)),
                plane,
                jnp.where(at == 7, after, pltpu.roll(plane, 7, 1)),
            )
            for b in range(3):
                for c in range(3):
                    hi, lo = split(shifted[c][b : b + 8].reshape(64, plane.shape[-1]))
                    hi_ref[3 * b + c, rows, :] = hi
                    lo_ref[3 * b + c, rows, :] = lo
            return carry

        lax.fori_loop(0, len(planes), body, 0)

    def window(hi_ref, lo_ref, t):
        t = jnp.int32(t)
        rows = pl.ds(pl.multiple_of(lax.div(t, 9) * 64, 64), 256)
        i = lax.rem(t, 9)
        return hi_ref[i, rows, :], lo_ref[i, rows, :]

    def kernel_grad(g):
        taps = min(4, 27 - 4 * g)
        for i in range(taps):
            d, at = divmod(26 - tap(4 * g + i), 9)
            rows = slice(64 * d, 64 * d + 256)
            upwin = wu_hi[at, rows, :], wu_lo[at, rows, :]
            res = dot3((vt_hi[...], vt_lo[...]), upwin, ((1,), (0,)))
            for block in range(8):
                for half in range(2):
                    part[g, block % 2, block // 2, 2 * i + half] = res[
                        32 * block : 32 * block + 32, 128 * half : 128 * half + 128
                    ]
        for i in range(taps, 4):
            for j in (2 * i, 2 * i + 1):
                part[g, :, :, j] = jnp.zeros((2, 4, 32, 128), F32)
        groups[g].pair()

    def products(first, last):
        def add(taps):
            out, grad = 0.0, 0.0
            for t in taps:
                k = split(k_f[t])
                out += dot3(window(wv_hi, wv_lo, t), k, ((1,), (0,)))
                grad += dot3(window(wu_hi, wu_lo, 26 - t), k, ((1,), (1,)))
            out_ref[...] += out
            vg_ref[...] += grad

        def body(i, carry):
            add((first + 2 * i, first + 2 * i + 1))
            return carry

        lax.fori_loop(0, (last - first) // 2, body, 0)
        if (last - first) % 2:
            add((last - 1,))

    def place(axis):
        return {"x": x, "y": y, "z": z}[axis]

    def away(axis, by):
        if axis == "x":
            return {"wa": step(w, 2 * by, 8)}
        return {"ha": step(y, by, 4)} if axis == "y" else {"dev": step(z, by, 8)}

    def direct(axis, chunk, recv):
        n = 8 if axis == "z" else 4
        return start(*(
            copy(chunk(step(place(axis), k, n)), recv.at[k - 1], away(axis, k)) for k in far_first(n)
        ))

    def direct_sum(axis, copies, chunk, recv):
        arrive(copies)
        total = chunk(place(axis))[...]
        for k in range(len(copies)):
            total = total + recv[k]
        return total

    def halves(ref, h):
        if len(ref.shape) == 4:
            return ref.at[:, pl.ds(4 * h, 4)]
        return ref.at[pl.ds(4 * h, 4)]

    def ring_1(axis, chunk, recv, recv_2):
        i = place(axis)
        far, above, below = (chunk(step(i, k, 4)) for k in (2, 1, -1))
        return start(
            copy(halves(far, 0), recv.at[0], away(axis, 1)),
            copy(halves(far, 1), recv.at[1], away(axis, -1)),
        ), start(
            copy(halves(above, 1), halves(recv_2.at[0], 1), away(axis, 1)),
            copy(halves(below, 0), halves(recv_2.at[1], 0), away(axis, -1)),
        )

    def ring_2(axis, copies, chunk, recv, stage, recv_2):
        arrive(copies)
        for h, by in ((0, 1), (1, -1)):
            stage[h] = halves(chunk(step(place(axis), by, 4)), h)[...] + recv[h]
        return start(
            copy(stage.at[0], halves(recv_2.at[0], 0), away(axis, 1)),
            copy(stage.at[1], halves(recv_2.at[1], 1), away(axis, -1)),
        )

    def rows_of(ref, k):
        rows = pl.ds(pl.multiple_of(k * 8, 8), 8)
        return ref.at[(slice(None),) * (len(ref.shape) - 2) + (rows,)]

    class Group:
        def __init__(self, g):
            self.g = g
            self.slot = SLOT[g]
            self.sum = summed.at[g]

        def pair(self):
            self.c = start(copy(part.at[self.g, 1 - core], pair.at[self.g], {"wa": w + 1 - 2 * core}))

        def add_pair(self):
            arrive(self.c)
            self.sum[...] = part[self.g, core] + pair[self.g]

    class PlaneGroup(Group):
        def __init__(self, g):
            super().__init__(g)
            self.first = FIRST[g]
            self.second = "y" if self.first == "x" else "x"
            n = FIRST[:g].count(self.first)
            i = 0 if self.first == "x" else 1
            self.r1, self.s2, self.r2 = r1[i].at[n], s2[i].at[n], r2[i].at[n]
            self.mid = mid[i].at[n]
            self.q1 = q1.at[self.slot]
            if self.first == "x":
                self.chunk_1 = lambda k: self.sum.at[k]
                self.chunk_2 = lambda k: rows_of(self.mid, k)
            else:
                self.chunk_1 = lambda k: rows_of(self.sum, k)
                self.chunk_2 = lambda k: self.mid.at[k]

        def e1(self):
            self.add_pair()
            self.c, self.near = ring_1(self.first, self.chunk_1, self.r1, self.r2)

        def e2(self):
            self.c = ring_2(self.first, self.c, self.chunk_1, self.r1, self.s2, self.r2)

        def e3(self):
            arrive(self.near)
            self.mid[...] = direct_sum(self.first, self.c, self.chunk_1, self.r2)
            self.c = direct(self.second, self.chunk_2, self.q1)

        def e4(self):
            low[self.slot] = direct_sum(self.second, self.c, self.chunk_2, self.q1)

    class DepthGroup(Group):
        def __init__(self, g):
            super().__init__(g)
            self.chunk_1 = lambda k: self.sum.at[:, k]
            self.chunk_2 = lambda k: zmid.at[k]
            self.chunk_3 = lambda k: rows_of(zlow, k)

        def e1(self):
            self.add_pair()
            self.c = direct("z", self.chunk_1, z1)

        def e2(self):
            zmid[...] = direct_sum("z", self.c, self.chunk_1, z1)
            self.c = direct("x", self.chunk_2, z2)

        def e3(self):
            zlow[...] = direct_sum("x", self.c, self.chunk_2, z2)
            self.c = direct("y", self.chunk_3, z3)

        def result(self):
            return direct_sum("y", self.c, self.chunk_3, z3)

    class Batch:
        def __init__(self, i):
            self.i = i
            lo, hi = BATCHES[i]
            self.depth_group = hi == SLOT[DEPTH] + 1
            self.n = hi - lo - (1 if self.depth_group else 0)
            self.lo = lo
            self.sums = pl.ds(lo, self.n)
            self.all = pl.ds(lo, hi - lo)

        def e6(self):
            self.c = start(*(
                copy(low.at[self.sums, step(z, k, 8)], rz.at[k - 1, self.sums], {"dev": step(z, k, 8)})
                for k in far_first(8)
            ))

        def e7(self):
            arrive(self.c)
            total = low[self.sums, z]
            for k in range(7):
                total = total + rz[k, self.sums]
            fin[self.sums] = total * factor
            if self.depth_group:
                fin[SLOT[DEPTH]] = groups[DEPTH].result() * factor
            agz_at = lambda k: agz.at[
                self.all, lax.div(k, 2), :, pl.ds(pl.multiple_of(lax.rem(k, 2) * 128, 128), 128)
            ]
            agz_at(z)[...] = fin[self.all]
            first = counter[0]
            start(*(copy(fin.at[self.all], agz_at(z), {"dev": step(z, k, 8)}) for k in far_first(8)))
            self.c = [
                self.landed(first + i, agz_at(step(z, -k, 8)), {"dev": step(z, k, 8)})
                for i, k in enumerate(far_first(8))
            ]

        def landed(self, i, slot, device):
            return pltpu.make_async_remote_copy(
                src_ref=slot, dst_ref=slot, send_sem=send_sem.at[i], recv_sem=recv_sem.at[i],
                device_id=device, device_id_type=MESH,
            )

        def e8(self):
            arrive(self.c)
            first = counter[0]
            here = agz.at[self.all]
            there = lambda k: rows_of(gathered.at[self.all], k)
            there(y)[...] = agz[self.all]
            start(*(copy(here, there(y), {"ha": step(y, k, 4)}) for k in far_first(4)))
            self.c = [
                self.landed(first + i, there(step(y, -k, 4)), {"ha": step(y, k, 4)})
                for i, k in enumerate(far_first(4))
            ]

        def e9(self):
            arrive(self.c)
            for u in range(27):
                if BATCHES[self.i][0] <= SLOT[u // 4] < BATCHES[self.i][1]:
                    kg_ref[tap(u)] = gathered[SLOT[u // 4], u % 4]

    groups = [(DepthGroup if FIRST[g] == "z" else PlaneGroup)(g) for g in range(GROUPS)]
    batches = [Batch(i) for i in range(len(BATCHES))]

    inner = [by for by in around if by[2] == 0]
    outer = [by for by in around if by[2] != 0]
    flat_u = send_halo(up_ref, pad_u, col_u, halo_u, inner[:2])
    deep_u = send_halo(up_ref, pad_u, col_u, halo_u, inner[2:])
    load_u.wait()
    cut_columns(pad_u, col_u)
    flat_u += send_halo(up_ref, pad_u, col_u, halo_u, outer[:6])
    deep_u += send_halo(up_ref, pad_u, col_u, halo_u, outer[6:])
    for c in k_copies:
        c.start()
    load_v.wait()
    cut_columns(pad_v, col_v)
    hi, lo = split(pad_v[1:5, 1:9].reshape(256, 256).T)
    vt_hi[...] = hi
    vt_lo[...] = lo
    out_ref[...] = jnp.zeros_like(out_ref)
    vg_ref[...] = jnp.zeros_like(vg_ref)
    arrive(flat_u)
    halos_v = send_halo(vol_ref, pad_v, col_v, halo_v, around)
    windows(pad_u, halo_u, wu_hi, wu_lo, range(1, 5))
    kernel_grad(0)
    kernel_grad(1)
    arrive(deep_u)
    windows(pad_u, halo_u, wu_hi, wu_lo, range(0, 6, 5))
    kernel_grad(2)
    groups[0].e1()
    kernel_grad(3)
    groups[1].e1()
    kernel_grad(4)
    groups[2].e1()
    groups[3].e1()
    kernel_grad(5)
    groups[4].e1()
    kernel_grad(6)
    groups[5].e1()
    groups[6].e1()
    groups[0].e2()
    groups[1].e2()
    arrive(halos_v)
    windows(pad_v, halo_v, wv_hi, wv_lo, range(6))
    for c in k_copies:
        c.wait()
    products(0, 4)
    groups[3].e2()
    groups[4].e2()
    products(4, 10)
    groups[5].e2()
    groups[6].e2()
    products(10, 12)
    groups[0].e3()
    groups[1].e3()
    products(12, 14)
    groups[3].e3()
    groups[4].e3()
    groups[2].e2()
    groups[5].e3()
    groups[6].e3()
    products(14, 18)
    groups[0].e4()
    groups[1].e4()
    batches[0].e6()
    groups[3].e4()
    groups[4].e4()
    batches[1].e6()
    groups[2].e3()
    groups[5].e4()
    groups[6].e4()
    batches[2].e6()
    products(18, 27)
    batches[0].e7()
    batches[1].e7()
    batches[2].e7()
    batches[0].e8()
    batches[1].e8()
    batches[2].e8()
    for batch in batches:
        batch.e9()
    assert counter[0] == N_SEM, counter[0]
    for c in sent:
        c.wait_send()


def store(out_in, vg_in, kg_in, out_ref, vg_ref, kg_ref, sem):
    copies = [
        pltpu.make_async_copy(src, dst, sem.at[i])
        for i, (src, dst) in enumerate(((kg_in, kg_ref), (out_in, out_ref), (vg_in, vg_ref)))
    ]
    for c in copies:
        c.start()
    for c in copies:
        c.wait()


def per_device(factor, volume, kernel_taps, upstream):
    nx, ny = FIRST.count("x"), FIRST.count("y")
    vmem = pltpu.VMEM
    scratch = [
        vmem((27, 256, 256), F32),
        vmem((6, 10, 8, 256), F32), vmem((6, 10, 8, 256), F32),
        vmem((2, 4, 8, 1, 256), F32), vmem((2, 4, 8, 1, 256), F32),
        vmem((2, 6, 10, 1, 256), F32), vmem((2, 6, 10, 1, 256), F32),
        vmem((9, 384, 256), BF16), vmem((9, 384, 256), BF16),
        vmem((9, 384, 256), BF16), vmem((9, 384, 256), BF16),
        vmem((256, 256), BF16), vmem((256, 256), BF16),
        vmem((GROUPS, 2, 4, 8, 32, 128), F32),
        vmem((GROUPS, 4, 8, 32, 128), F32),
        vmem((GROUPS, 4, 8, 32, 128), F32),
        [vmem((nx, 2, 4, 32, 128), F32), vmem((ny, 2, 4, 4, 8, 128), F32)],
        [vmem((nx, 2, 4, 32, 128), F32), vmem((ny, 2, 4, 4, 8, 128), F32)],
        [vmem((nx, 2, 8, 32, 128), F32), vmem((ny, 2, 4, 8, 8, 128), F32)],
        [vmem((nx, 8, 32, 128), F32), vmem((ny, 4, 8, 8, 128), F32)],
        vmem((GROUPS, 3, 8, 8, 128), F32),
        vmem((GROUPS, 8, 8, 128), F32),
        vmem((7, GROUPS, 8, 128), F32),
        vmem((GROUPS, 8, 128), F32),
        vmem((GROUPS, 4, 8, 256), F32),
        vmem((GROUPS, 4, 32, 256), F32),
        vmem((7, 4, 32, 128), F32), vmem((4, 32, 128), F32),
        vmem((3, 32, 128), F32), vmem((32, 128), F32),
        vmem((3, 8, 128), F32),
        pltpu.SemaphoreType.DMA((3,)),
        pltpu.SemaphoreType.DMA((2,)),
        pltpu.SemaphoreType.DMA((N_SEM,)),
        pltpu.SemaphoreType.DMA((N_SEM,)),
    ]
    here = pl.BlockSpec(memory_space=pl.ANY)
    held = pl.BlockSpec(memory_space=pltpu.VMEM)
    output, volume_grad, kg = pl.pallas_call(
        functools.partial(kernel, factor),
        out_shape=(vmem((256, 256), F32), vmem((256, 256), F32), vmem((27, 32, 256), F32)),
        in_specs=[here] * 3,
        out_specs=(held,) * 3,
        scratch_shapes=scratch,
        compiler_params=pltpu.CompilerParams(
            collective_id=0, has_side_effects=True, vmem_limit_bytes=56 * 2**20
        ),
    )(volume, upstream, jnp.transpose(kernel_taps, (1, 0, 2)))
    results = [
        pltpu.with_memory_space_constraint(r, pltpu.VMEM) for r in (output, volume_grad, kg)
    ]
    output, volume_grad, kg = pl.pallas_call(
        store,
        out_shape=tuple(jax.ShapeDtypeStruct(r.shape, F32) for r in results),
        in_specs=[held] * 3,
        out_specs=(here,) * 3,
        scratch_shapes=[pltpu.SemaphoreType.DMA((3,))],
    )(*results)
    return (
        output.reshape(volume.shape),
        volume_grad.reshape(volume.shape),
        jnp.transpose(kg, (1, 0, 2)),
    )


def solution(mesh):
    cells = 256 * mesh.shape["dev"] * mesh.shape["ha"] * mesh.shape["wa"]
    place = P("dev", "ha", "wa", None)
    return jax.shard_map(
        functools.partial(per_device, 1.0 / math.sqrt(cells)),
        mesh=mesh,
        in_specs=(place, P(), place),
        out_specs=(place, place, P("wa", None, None)),
        check_vma=False,
    )
```
